32 devices in a mesh: groups: 2 (over y), seq: 16 (over z, x, core).
Axes of the slice: x: 2, y: 2, z: 4, core: 2. Of those that a mesh axis runs over, the one named last changes fastest.
Arguments:
- q_lin: bfloat16 [16384, 128], P(('groups', 'seq')), parts along dimension 0, may hold values from -6 to 6
- k_lin: bfloat16 [16384, 128], P(('groups', 'seq')), parts along dimension 0, may hold values from -6 to 6
- v_lin: bfloat16 [16384, 512], P(('groups', 'seq')), parts along dimension 0, may hold values from -6 to 6
- q_win: bfloat16 [16384, 2048], P(('groups', 'seq')), parts along dimension 0, may hold values from -10 to 10
- k_win: bfloat16 [16384, 2048], P(('groups', 'seq')), parts along dimension 0, may hold values from -10 to 10
- v_win: bfloat16 [16384, 2048], P(('groups', 'seq')), parts along dimension 0, may hold values from -6 to 6
Outputs:
- lin_out: bfloat16 [16384, 512], P(('groups', 'seq')), parts along dimension 0
- win_out: bfloat16 [16384, 2048], P(('groups', 'seq')), parts along dimension 0
The draws below stay inside these ranges and needn't reach their ends.
There are 2 independent parts, one for each index of `groups`. The reference program is written for one: setup_inputs(seed, part) draws one part's arguments, and reference() takes and returns one part's arrays. A program takes and returns all parts, laid end to end along the dimension named above; each array names one. Nothing has to cross between parts.
All inputs are finite; a program needn't handle non-finite values.
Results may differ from the reference program's by a relative error of at most 0.005.
Values may be sent and summed in bfloat16 or wider, within the bound.
No kernel may reach another device: no remote copies, remote signals or barrier semaphores. Data moves between devices by JAX's collectives and lax.ppermute only.
A program may use at most 192 MiB of HBM per device.

```python
import math
import jax
import jax.numpy as jnp
from jax import lax

HEADS = 8
KDIM = 16
VDIM = 64
WHEADS = 16
WDIM = 128
WINDOW = 64
TOK_DEV = 512
TOKENS = 8192
FEATS = 273


def draw_v_lin(key, part):
    noise_key, offset_key = jax.random.split(jax.random.fold_in(key, 11))
    block_count = (TOKENS + 255) // 256
    noise = jax.random.truncated_normal(noise_key, -3.0, 3.0, (TOKENS, HEADS * VDIM), jnp.float32)
    table = jax.random.uniform(offset_key, (block_count, HEADS * VDIM), jnp.float32, -2.0, 2.0)
    offset = jnp.repeat(table, 256, axis=0)[:TOKENS]
    return (noise + offset).astype(jnp.bfloat16)


def window_pair(key, aligned):
    base = jax.random.fold_in(key, 7)
    first_key, second_key, sign_key, query_key, strong_key = jax.random.split(base, 5)
    shape = (TOKENS, WHEADS, WDIM)
    queries = jax.random.truncated_normal(first_key, -4.0, 4.0, shape, jnp.float32)
    keys = jax.random.truncated_normal(second_key, -4.0, 4.0, shape, jnp.float32)
    if aligned:
        direction = jnp.where(jax.random.bernoulli(sign_key, 0.5, (1, WHEADS, WDIM)), 1.0, -1.0)
        query_strength = jax.random.uniform(query_key, (TOKENS, WHEADS, 1), jnp.float32, 0.0, 6.0)
        key_strength = 3.5 + 0.15 * jax.random.truncated_normal(strong_key, -3.0, 3.0, (TOKENS, WHEADS, 1), jnp.float32)
        queries = queries + query_strength * direction
        keys = keys + key_strength * direction
    return (queries.reshape(TOKENS, WHEADS * WDIM), keys.reshape(TOKENS, WHEADS * WDIM))


def draw_q_win(key, part):
    pair = window_pair(key, False)
    return pair[0].astype(jnp.bfloat16)


def draw_k_win(key, part):
    pair = window_pair(key, False)
    return pair[1].astype(jnp.bfloat16)


def shard_levels(own_key, extent, shards, least, largest):
    level, own = 1.0, jax.random.fold_in(own_key, 6)
    for dim, blocks in shards:
        steps = jnp.exp(jax.random.uniform(jax.random.fold_in(own, dim), (blocks,), jnp.float32, least / len(shards), largest / len(shards)))
        level = level * jnp.repeat(steps, extent[dim] // blocks).reshape([-1 if axis == dim else 1 for axis in range(len(extent))])
    return level


def bell_draw(stream_key, shape, spread, limit, cuts=(), kind=jnp.bfloat16):
    gain = shard_levels(stream_key, shape, cuts, -0.22, 0.18) if cuts else 1.0
    entries = jax.random.normal(stream_key, shape, jnp.float32) * spread * gain
    return jnp.minimum(jnp.maximum(entries, -limit), limit).astype(kind)


def setup_inputs(seed: int = 0, part: int = 0) -> dict:
    splits = jax.random.split(jax.random.key(seed), 7)
    own_keys = jax.random.split(jax.random.fold_in(splits[6], part), 7)
    q_lin = bell_draw(own_keys[0], (TOKENS, HEADS * KDIM), 1.0, 6.0, ((0, 16),))
    k_lin = bell_draw(own_keys[1], (TOKENS, HEADS * KDIM), 1.0, 6.0, ((0, 16),))
    v_lin = draw_v_lin(jax.random.fold_in(jax.random.fold_in(splits[6], part), 71), part)
    q_win = draw_q_win(jax.random.fold_in(jax.random.fold_in(splits[6], part), 71), part)
    k_win = draw_k_win(jax.random.fold_in(jax.random.fold_in(splits[6], part), 71), part)
    v_win = bell_draw(own_keys[5], (TOKENS, WHEADS * WDIM), 1.0, 6.0, ((0, 16),))
    return dict(q_lin=q_lin, k_lin=k_lin, v_lin=v_lin, q_win=q_win, k_win=k_win, v_win=v_win)


highest = lax.Precision.HIGHEST

def full_features(scaled):
    tok_count = scaled.shape[0]
    ones_part = jnp.ones((tok_count, HEADS, 1), jnp.float32)
    square = (scaled[:, :, :, None] * scaled[:, :, None, :]).reshape(tok_count, HEADS, KDIM * KDIM) * (1.0 / math.sqrt(2.0))
    return jnp.concatenate([ones_part, scaled, square], axis=2)

def linear_part(q_lin, k_lin, v_lin):
    block = math.gcd(TOK_DEV, 128)
    count = TOKENS // block
    root = float(KDIM) ** 0.25
    queries = q_lin.astype(jnp.float32).reshape(count, block, HEADS, KDIM) / root
    keys = k_lin.astype(jnp.float32).reshape(count, block, HEADS, KDIM) / root
    values = v_lin.astype(jnp.float32).reshape(count, block, HEADS, VDIM)
    position = jnp.arange(block)
    causal = position[:, None] >= position[None, :]

    def advance(carry, pieces):
        state, norm_sum = carry
        block_q, block_k, block_v = pieces
        feats_q = full_features(block_q)
        feats_k = full_features(block_k)
        similar = jnp.einsum('chk,shk->hcs', block_q, block_k, precision=highest)
        kernel = jnp.where(causal[None], 1.0 + similar + 0.5 * similar * similar, 0.0)
        numerator = jnp.einsum('hcs,shv->chv', kernel, block_v, precision=highest)
        numerator = numerator + jnp.einsum('chf,hfv->chv', feats_q, state, precision=highest)
        denominator = lax.optimization_barrier(jnp.sum(kernel, axis=2)).T + jnp.einsum('chf,hf->ch', feats_q, norm_sum, precision=highest)
        result = (numerator / denominator[:, :, None]).reshape(block, HEADS * VDIM).astype(jnp.bfloat16)
        state = state + jnp.einsum('chf,chv->hfv', feats_k, block_v, precision=highest)
        norm_sum = norm_sum + lax.optimization_barrier(jnp.sum(feats_k, axis=0))
        return ((state, norm_sum), result)
    start = (jnp.zeros((HEADS, FEATS, VDIM), jnp.float32), jnp.zeros((HEADS, FEATS), jnp.float32))
    final, outputs = lax.scan(advance, start, (queries, keys, values))
    return outputs.reshape(TOKENS, HEADS * VDIM)

def window_part(q_win, k_win, v_win):
    count = TOKENS // WINDOW
    queries = q_win.reshape(count, WINDOW, WHEADS, WDIM)
    padding = jnp.zeros((WINDOW, WHEADS * WDIM), k_win.dtype)
    keys_pad = jnp.concatenate([padding, k_win], axis=0).reshape(TOKENS + WINDOW, WHEADS, WDIM)
    vals_pad = jnp.concatenate([padding, v_win], axis=0).reshape(TOKENS + WINDOW, WHEADS, WDIM)
    query_pos = jnp.arange(WINDOW)[:, None]
    key_pos = jnp.arange(2 * WINDOW)[None, :]

    def one_block(index):
        start = (index * WINDOW).astype(jnp.int32)
        block_q = lax.dynamic_index_in_dim(queries, index, 0, keepdims=False)
        block_k = lax.dynamic_slice_in_dim(keys_pad, start, 2 * WINDOW, 0)
        block_v = lax.dynamic_slice_in_dim(vals_pad, start, 2 * WINDOW, 0)
        scores = jnp.einsum('thd,shd->hts', block_q.astype(jnp.float32), block_k.astype(jnp.float32)) / math.sqrt(WDIM)
        allowed = (key_pos > query_pos) & (key_pos <= query_pos + WINDOW) & (start + key_pos >= WINDOW)
        scores = jnp.where(allowed[None], scores, -jnp.inf)
        peak = lax.optimization_barrier(jnp.max(scores, axis=2, keepdims=True))
        expo = jnp.exp(scores - peak)
        weights = (expo / lax.optimization_barrier(jnp.sum(expo, axis=2, keepdims=True))).astype(jnp.bfloat16)
        result = jnp.einsum('hts,shd->thd', weights.astype(jnp.float32), block_v.astype(jnp.float32))
        return result.astype(jnp.bfloat16).reshape(WINDOW, WHEADS * WDIM)
    blocks = lax.map(one_block, jnp.arange(count, dtype=jnp.int32))
    return blocks.reshape(TOKENS, WHEADS * WDIM)

def reference(q_lin, k_lin, v_lin, q_win, k_win, v_win):
    lin_out = linear_part(q_lin, k_lin, v_lin)
    win_out = window_part(q_win, k_win, v_win)
    return (lin_out, win_out)
```

```python
import math

import jax
import jax.numpy as jnp
from jax import lax
from jax.experimental import pallas as pl
from jax.experimental.pallas import tpu as pltpu
from jax.sharding import PartitionSpec as P

HEADS = 8
KDIM = 16
VDIM = 64
WHEADS = 16
WDIM = 128
WINDOW = 64

BF = jnp.bfloat16
F32 = jnp.float32
BLOCKS = 10
PAIRS = BLOCKS // 2
MAIN = PAIRS * 64
ROWS = MAIN + 16
STEP = 256
COEF = (1 / 32,) + (1 / 16,) * 7 + (1 / 32, 1 / 4)
VMEM = pl.BlockSpec(memory_space=pltpu.VMEM)


def lanes(shape):
    return lax.broadcasted_iota(jnp.int32, shape, len(shape) - 1)


def rows_of(shape):
    return lax.broadcasted_iota(jnp.int32, shape, len(shape) - 2)


def feature(x, d):
    if d == 9:
        return x
    if d == 0:
        return x * x
    low = lanes(x.shape) % KDIM < KDIM - d
    other = jnp.where(low, pltpu.roll(x, 128 - d, 1), pltpu.roll(x, KDIM - d, 1))
    return x * other


def halves(first, second):
    left = lanes(first.shape) < 64
    return (
        jnp.where(left, first, pltpu.roll(second, 64, 1)),
        jnp.where(left, pltpu.roll(first, 64, 1), second),
    )


def put_features(x, coef, fa, fb):
    sums = []
    for p in range(PAIRS):
        blocks = [feature(x, d) * coef[d] for d in (2 * p, 2 * p + 1)]
        sums.append([jnp.sum(b, axis=0, keepdims=True) for b in blocks])
        a, b = halves(*blocks)
        fa[:, p * 128 : (p + 1) * 128] = a.astype(BF)
        fb[:, p * 128 : (p + 1) * 128] = b.astype(BF)
    return sums


def state_kernel(k_hbm, v_hbm, s_ref, fa, fb, kbuf, vbuf, sems):
    copies = [
        pltpu.make_async_copy(src, dst, sems.at[n])
        for n, (src, dst) in enumerate(((k_hbm, kbuf), (v_hbm, vbuf)))
    ]
    for copy in copies:
        copy.start()
    copies[0].wait()
    sums = put_features(kbuf[...].astype(F32), (1.0,) * BLOCKS, fa, fb)
    zs = [halves(*pair) for pair in sums]
    copies[1].wait()
    v = vbuf[...]
    vsum = jnp.sum(v.astype(F32), axis=0, keepdims=True)
    left = lanes((64, 128)) < 64
    even = (rows_of((64, 128)) // KDIM) % 2 == 0
    for half, f in ((0, fa), (1, fb)):
        r = lax.dot_general(
            f[...],
            v[:, half * 256 : (half + 1) * 256],
            (((0,), (0,)), ((), ())),
            preferred_element_type=F32,
        )
        for p in range(PAIRS):
            pieces = []
            for par in range(2):
                at = p * 128 + par * 64
                z = jnp.concatenate(
                    [r[at : at + 32, :128], r[at + 32 : at + 64, 128:]], axis=0
                )
                keep = even if par == 0 else jnp.logical_not(even)
                pieces.append(jnp.where(keep, z, pltpu.roll(z, 64, 1)))
            s_ref[half, p * 64 : (p + 1) * 64, :] = jnp.where(left, *pieces).astype(BF)
        aux = [z[half] for z in zs]
        aux += [vsum[:, half * 256 + t * 128 : half * 256 + (t + 1) * 128] for t in range(2)]
        aux.append(jnp.zeros((ROWS - MAIN - PAIRS - 2, 128), F32))
        s_ref[half, MAIN:, :] = jnp.concatenate(aux, axis=0).astype(BF)


def query_kernel(q_ref, fa, fb):
    put_features(q_ref[...].astype(F32), COEF, fa, fb)


def local_kernel(q_ref, k_ref, v_ref, num_ref, den_ref):
    tok = q_ref.shape[0]
    step = STEP
    k = k_ref[...]
    lane = lanes((step, 128))
    left = lane < 64
    left_all = lanes((tok, 128)) < 64
    causal = rows_of((step, step)) >= lanes((step, step))
    one = jnp.ones((tok, 128), BF)
    for t in range(HEADS // 2):
        vt = v_ref[:, t * 128 : (t + 1) * 128]
        aug = (jnp.where(left_all, vt, one), jnp.where(left_all, one, vt))
        for r in range(tok // step):
            q = q_ref[r * step : (r + 1) * step, :]
            outs = []
            for e in range(2):
                qm = jnp.where(lane // KDIM == 2 * t + e, q, jnp.zeros_like(q))
                end = (r + 1) * step
                u = lax.dot_general(
                    qm, k[:end, :], (((1,), (1,)), ((), ())), preferred_element_type=F32
                )
                w = u + 4.0
                w = w * w * (1 / 32) + 0.5
                diag = jnp.where(causal, w[:, r * step :], 0.0).astype(BF)
                if r:
                    w = jnp.concatenate([w[:, : r * step].astype(BF), diag], axis=1)
                else:
                    w = diag
                outs.append(jnp.dot(w, aug[e][:end, :], preferred_element_type=F32))
            num_ref[r * step : (r + 1) * step, t * 128 : (t + 1) * 128] = jnp.where(
                left, outs[0], outs[1]
            )
            den_ref[r * step : (r + 1) * step, t * 128 : (t + 1) * 128] = pltpu.roll(
                jnp.where(left, outs[1], outs[0]), 64, 1
            )


def finish_kernel(fa, fb, own_ref, other_ref, peer_ref, num_ref, den_ref, o_ref, pa, pb):
    tok = fa.shape[0]
    me = lax.axis_index("seq")
    second = me % 2 == 1
    own = own_ref[...].astype(F32)
    other = other_ref[...].astype(F32)
    left = lanes((64, 128)) < 64
    row = rows_of((64, 128)) // KDIM
    col = lanes((64, 128)) // VDIM
    span = ((rows_of((256, 256)) // KDIM) % 4 == lanes((256, 256)) // VDIM).astype(BF)
    count = (me * tok).astype(F32)
    for half, f, dst in ((0, fa, pa), (1, fb, pb)):
        state = jnp.where(second == (half == 1), own, other)
        state = state + jnp.where(second, peer_ref[half].astype(F32), 0.0)
        for p in range(PAIRS):
            c = state[p * 64 : (p + 1) * 64, :]
            turned = pltpu.roll(c, 64, 1)
            for par in range(2):
                base = jnp.where(left, c, turned) if par == 0 else jnp.where(left, turned, c)
                at = p * 128 + par * 64
                for t in range(2):
                    dst[at : at + 64, t * 128 : (t + 1) * 128] = jnp.where(
                        row == col + 2 * t, base, 0.0
                    ).astype(BF)
        cols = slice(half * 256, (half + 1) * 256)
        acc = jnp.zeros((tok, 128), F32)
        for p in range(PAIRS):
            acc = acc + f[:, p * 128 : (p + 1) * 128].astype(F32) * state[MAIN + p : MAIN + p + 1, :]
        high = acc.astype(BF)
        both = jnp.concatenate([high, (acc - high.astype(F32)).astype(BF)], axis=1)
        den = jnp.dot(both, span, preferred_element_type=F32) + den_ref[:, cols] + count
        at = MAIN + PAIRS
        vsum = jnp.concatenate([state[at : at + 1, :], state[at + 1 : at + 2, :]], axis=1)
        num = jnp.dot(f[...], dst[...], preferred_element_type=F32)
        o_ref[:, cols] = ((num + num_ref[:, cols] + vsum) / den).astype(BF)


SCALE = 1.0 / (math.sqrt(WDIM) * math.log(2.0))
QB = 2 * WINDOW


def masks():
    row, lane = rows_of((QB, QB)), lanes((QB, QB))
    earlier = (row < WINDOW) & (lane >= WINDOW)
    key = jnp.where(earlier, lane, lane + QB) - QB
    return earlier, key, (key <= row) & (key > row - WINDOW)


def attend(blocks, earlier, bias):
    s = jnp.stack(
        [
            lax.dot_general(q, k, (((1,), (1,)), ((), ())), preferred_element_type=F32)
            for q, k, v in blocks
        ]
    )
    s = jnp.where(earlier, s[:, :, :QB], s[:, :, QB:]) * SCALE + bias
    e = jnp.exp2(s - jnp.max(s, axis=2, keepdims=True))
    inverse = 1.0 / jnp.sum(e, axis=2, keepdims=True)
    e = jnp.concatenate([jnp.where(earlier, e, 0.0), jnp.where(earlier, 0.0, e)], axis=2).astype(BF)
    return [
        (jnp.dot(e[n], v, preferred_element_type=F32) * inverse[n]).astype(BF)
        for n, (q, k, v) in enumerate(blocks)
    ]


def window_kernel(q_ref, k_ref, v_ref, *refs):
    o_ref = refs[-1]
    earlier, _, allowed = masks()
    bias = jnp.where(allowed, 0.0, -jnp.inf)
    starts = range(QB, q_ref.shape[0], QB)
    for h in range(q_ref.shape[1] // WDIM):
        cols = slice(h * WDIM, (h + 1) * WDIM)
        outs = attend(
            [
                (q_ref[at : at + QB, cols], k_ref[at - QB : at + QB, cols], v_ref[at - QB : at + QB, cols])
                for at in starts
            ],
            earlier,
            bias,
        )
        for at, out in zip(starts, outs):
            o_ref[at : at + QB, cols] = out


def edge_kernel(q_ref, k_ref, v_ref, h_ref, whole_ref, o_ref):
    first = lax.axis_index("seq") == 0
    earlier, key, allowed = masks()
    bias = jnp.where(allowed & ((key >= 0) | jnp.logical_not(first)), 0.0, -jnp.inf)
    for h in range(q_ref.shape[1] // WDIM):
        cols = slice(h * WDIM, (h + 1) * WDIM)
        kh, vh = h_ref[:WINDOW, cols], h_ref[WINDOW:, cols]
        k = jnp.concatenate([kh, kh, k_ref[:, cols]], axis=0)
        v = jnp.concatenate([vh, vh, v_ref[:, cols]], axis=0)
        o_ref[:, cols] = attend([(q_ref[:, cols], k, v)], earlier, bias)[0]


def halo_kernel(k_ref, v_ref, o_ref, sems):
    tok = k_ref.shape[0]
    copies = [
        pltpu.make_async_copy(
            ref.at[pl.ds(tok - WINDOW, WINDOW)], o_ref.at[pl.ds(n * WINDOW, WINDOW)], sems.at[n]
        )
        for n, ref in enumerate((k_ref, v_ref))
    ]
    for copy in copies:
        copy.start()
    for copy in copies:
        copy.wait()


def call(kernel, out, *args, flops=0, nbytes=0, vmem=16, **kw):
    return pl.pallas_call(
        kernel,
        out_shape=out,
        cost_estimate=pl.CostEstimate(flops=flops, bytes_accessed=nbytes, transcendentals=0),
        compiler_params=pltpu.CompilerParams(vmem_limit_bytes=vmem << 20),
        **kw,
    )(*args)


def exchange(x, step):
    count = lax.axis_size("seq")
    return lax.ppermute(x, "seq", [(i, i ^ step) for i in range(count)])


def shape(*dims, dtype=BF):
    return jax.ShapeDtypeStruct(dims, dtype)


def body(q_lin, k_lin, v_lin, q_win, k_win, v_win):
    tok = q_lin.shape[0]
    count = lax.axis_size("seq")
    assert count & (count - 1) == 0 and count > 1
    me = lax.axis_index("seq")
    second = me % 2 == 1
    wide = WHEADS * WDIM
    hbm = pl.BlockSpec(memory_space=pltpu.HBM)
    feats = pltpu.VMEM((tok, PAIRS * 128), BF)

    def window(group, groups, earlier):
        cols = wide // groups
        width = 512
        block = pl.BlockSpec((tok, width), lambda i: (0, group * (cols // width) + i))
        extra = () if earlier is None else (earlier,)
        return call(
            window_kernel,
            shape(tok, wide),
            q_win,
            k_win,
            v_win,
            *extra,
            grid=(cols // width,),
            in_specs=[block] * 3 + [hbm] * len(extra),
            out_specs=block,
            input_output_aliases={3: 0} if extra else {},
            flops=(1 << 31) // groups,
            nbytes=(8 << 20) // groups,
        )

    def halo():
        edge = call(
            halo_kernel,
            shape(2 * WINDOW, wide),
            k_win,
            v_win,
            in_specs=[hbm, hbm],
            out_specs=VMEM,
            scratch_shapes=[pltpu.SemaphoreType.DMA((2,))],
            nbytes=1 << 20,
        )
        return lax.ppermute(edge, "seq", [(i, (i + 1) % count) for i in range(count)])

    def local(q, k, v):
        return call(
            local_kernel,
            (shape(tok, HEADS * VDIM, dtype=F32),) * 2,
            q,
            k,
            v,
            in_specs=[VMEM] * 3,
            out_specs=(VMEM, VMEM),
            flops=1 << 31,
            nbytes=3 << 20,
        )

    edge = halo()
    state = call(
        state_kernel,
        shape(2, ROWS, 128),
        k_lin,
        v_lin,
        in_specs=[hbm] * 2,
        out_specs=VMEM,
        scratch_shapes=[feats] * 2
        + [pltpu.VMEM(k_lin.shape, BF), pltpu.VMEM(v_lin.shape, BF), pltpu.SemaphoreType.DMA((2,))],
        flops=1 << 30,
        nbytes=1 << 20,
    )
    peer = exchange(state, 1)
    qa, qb = call(
        query_kernel,
        (shape(tok, PAIRS * 128),) * 2,
        q_lin,
        in_specs=[VMEM],
        out_specs=(VMEM, VMEM),
        flops=1 << 28,
        nbytes=1 << 20,
    )
    both = state.astype(F32) + peer.astype(F32)
    carried = jnp.where(second, both[1], both[0])
    before = jnp.zeros_like(carried)
    win = None
    step, turn = 2, 0
    lin = (q_lin, k_lin, v_lin)
    num = den = None
    while step < count:
        if turn == 0:
            carried, lin = lax.optimization_barrier((carried, lin))
        got = exchange(carried.astype(BF), step)
        if turn == 0:
            num, den = local(*lin)
            got, num, den = lax.optimization_barrier((got, num, den))
        elif turn < 3:
            win = window(turn - 1, 2, win)
            got, win = lax.optimization_barrier((got, win))
        got = got.astype(F32)
        before = before + jnp.where((me & step) != 0, got, 0.0)
        carried = carried + got
        step *= 2
        turn += 1
    own = before.astype(BF)
    other = exchange(own, 1)
    top = pl.BlockSpec((QB, wide), lambda i: (0, 0))
    win_out = call(
        edge_kernel,
        shape(tok, wide),
        q_win,
        k_win,
        v_win,
        edge,
        win,
        grid=(1,),
        in_specs=[top] * 4 + [hbm],
        out_specs=top,
        input_output_aliases={4: 0},
        flops=1 << 28,
        nbytes=1 << 20,
    )
    lin_out = call(
        finish_kernel,
        shape(tok, HEADS * VDIM),
        qa,
        qb,
        own,
        other,
        peer,
        num,
        den,
        in_specs=[VMEM] * 7,
        out_specs=VMEM,
        scratch_shapes=[pltpu.VMEM((PAIRS * 128, 256), BF)] * 2,
        flops=1 << 30,
        nbytes=3 << 20,
    )
    return (lin_out, win_out)


def solution(mesh):
    spec = P(("groups", "seq"), None)
    return jax.shard_map(
        body, mesh=mesh, in_specs=(spec,) * 6, out_specs=(spec, spec), check_vma=False
    )
```

```python
import math

import jax
import jax.numpy as jnp
from jax import lax
from jax.experimental import pallas as pl
from jax.experimental.pallas import tpu as pltpu
from jax.sharding import PartitionSpec as P

HEADS = 8
KDIM = 16
VDIM = 64
WHEADS = 16
WDIM = 128
WINDOW = 64

BF = jnp.bfloat16
F32 = jnp.float32
BLOCKS = 10
PAIRS = BLOCKS // 2
MAIN = PAIRS * 64
ROWS = MAIN + 16
STEP = 256
GROUP = 4
COEF = (1 / 32,) + (1 / 16,) * 7 + (1 / 32, 1 / 4)
VMEM = pl.BlockSpec(memory_space=pltpu.VMEM)


def lanes(shape):
    return lax.broadcasted_iota(jnp.int32, shape, len(shape) - 1)


def rows_of(shape):
    return lax.broadcasted_iota(jnp.int32, shape, len(shape) - 2)


def feature(x, d):
    if d == 9:
        return x
    if d == 0:
        return x * x
    low = lanes(x.shape) % KDIM < KDIM - d
    other = jnp.where(low, pltpu.roll(x, 128 - d, 1), pltpu.roll(x, KDIM - d, 1))
    return x * other


def halves(first, second):
    left = lanes(first.shape) < 64
    return (
        jnp.where(left, first, pltpu.roll(second, 64, 1)),
        jnp.where(left, pltpu.roll(first, 64, 1), second),
    )


def put_features(x, coef, fa, fb):
    sums = []
    for p in range(PAIRS):
        blocks = [feature(x, d) * coef[d] for d in (2 * p, 2 * p + 1)]
        sums.append([jnp.sum(b, axis=0, keepdims=True) for b in blocks])
        a, b = halves(*blocks)
        fa[:, p * 128 : (p + 1) * 128] = a.astype(BF)
        fb[:, p * 128 : (p + 1) * 128] = b.astype(BF)
    return sums


def load_kernel(q_hbm, k_hbm, v_hbm, kw_hbm, vw_hbm, edge_ref, q_ref, k_ref, v_ref, sems):
    last = pl.ds(kw_hbm.shape[0] - WINDOW, WINDOW)
    moves = (
        (kw_hbm.at[last], edge_ref.at[pl.ds(0, WINDOW)]),
        (vw_hbm.at[last], edge_ref.at[pl.ds(WINDOW, WINDOW)]),
        (k_hbm, k_ref),
        (v_hbm, v_ref),
        (q_hbm, q_ref),
    )
    copies = [pltpu.make_async_copy(src, dst, sems.at[n]) for n, (src, dst) in enumerate(moves)]
    for copy in copies:
        copy.start()
    for copy in copies:
        copy.wait()


def state_kernel(k_ref, v_ref, s_ref, fa, fb):
    sums = put_features(k_ref[...].astype(F32), (1.0,) * BLOCKS, fa, fb)
    zs = [halves(*pair) for pair in sums]
    v = v_ref[...]
    vsum = jnp.sum(v.astype(F32), axis=0, keepdims=True)
    left = lanes((64, 128)) < 64
    even = (rows_of((64, 128)) // KDIM) % 2 == 0
    for half, f in ((0, fa), (1, fb)):
        r = lax.dot_general(
            f[...],
            v[:, half * 256 : (half + 1) * 256],
            (((0,), (0,)), ((), ())),
            preferred_element_type=F32,
        )
        for p in range(PAIRS):
            pieces = []
            for par in range(2):
                at = p * 128 + par * 64
                z = jnp.concatenate(
                    [r[at : at + 32, :128], r[at + 32 : at + 64, 128:]], axis=0
                )
                keep = even if par == 0 else jnp.logical_not(even)
                pieces.append(jnp.where(keep, z, pltpu.roll(z, 64, 1)))
            s_ref[half, p * 64 : (p + 1) * 64, :] = jnp.where(left, *pieces).astype(BF)
        aux = [z[half] for z in zs]
        aux += [vsum[:, half * 256 + t * 128 : half * 256 + (t + 1) * 128] for t in range(2)]
        aux.append(jnp.zeros((ROWS - MAIN - PAIRS - 2, 128), F32))
        s_ref[half, MAIN:, :] = jnp.concatenate(aux, axis=0).astype(BF)


def query_kernel(q_ref, fa, fb, done):
    done[...] = jnp.zeros_like(done)
    put_features(q_ref[...].astype(F32), COEF, fa, fb)


def local_kernel(q_ref, k_ref, v_ref, num_ref, den_ref, done):
    done[...] = jnp.zeros_like(done)
    tok = q_ref.shape[0]
    step = STEP
    k = k_ref[...]
    lane = lanes((step, 128))
    left = lane < 64
    left_all = lanes((tok, 128)) < 64
    causal = rows_of((step, step)) >= lanes((step, step))
    one = jnp.ones((tok, 128), BF)
    for r in range(tok // step):
        rows, end = slice(r * step, (r + 1) * step), (r + 1) * step
        q = q_ref[rows, :]
        for t0 in range(0, HEADS // 2, 2):
            places = [(t, e) for t in (t0, t0 + 1) for e in range(2)]
            kernels = []
            for t, e in places:
                qm = jnp.where(lane // KDIM == 2 * t + e, q, jnp.zeros_like(q))
                u = lax.dot_general(
                    qm, k[:end, :], (((1,), (1,)), ((), ())), preferred_element_type=F32
                )
                kernels.append(u + 4.0)
            outs = []
            for w, (t, e) in zip(kernels, places):
                w = w * w * (1 / 32) + 0.5
                diag = jnp.where(causal, w[:, r * step :], 0.0).astype(BF)
                if r:
                    diag = jnp.concatenate([w[:, : r * step].astype(BF), diag], axis=1)
                v = v_ref[:, t * 128 : (t + 1) * 128]
                aug = jnp.where(left_all, one, v) if e else jnp.where(left_all, v, one)
                outs.append(jnp.dot(diag, aug[:end, :], preferred_element_type=F32))
            for n in range(2):
                cols = slice((t0 + n) * 128, (t0 + n + 1) * 128)
                a, b = outs[2 * n : 2 * n + 2]
                num_ref[rows, cols] = jnp.where(left, a, b)
                den_ref[rows, cols] = pltpu.roll(jnp.where(left, b, a), 64, 1)


def finish_kernel(fa, fb, own_ref, other_ref, peer_ref, num_ref, den_ref, o_ref, pa, pb):
    tok = fa.shape[0]
    me = lax.axis_index("seq")
    second = me % 2 == 1
    own = own_ref[...].astype(F32)
    other = other_ref[...].astype(F32)
    left = lanes((64, 128)) < 64
    row = rows_of((64, 128)) // KDIM
    col = lanes((64, 128)) // VDIM
    span = ((rows_of((256, 256)) // KDIM) % 4 == lanes((256, 256)) // VDIM).astype(BF)
    count = (me * tok).astype(F32)
    for half, f, dst in ((0, fa, pa), (1, fb, pb)):
        state = jnp.where(second == (half == 1), own, other)
        state = state + jnp.where(second, peer_ref[half].astype(F32), 0.0)
        for p in range(PAIRS):
            c = state[p * 64 : (p + 1) * 64, :]
            turned = pltpu.roll(c, 64, 1)
            for par in range(2):
                base = jnp.where(left, c, turned) if par == 0 else jnp.where(left, turned, c)
                at = p * 128 + par * 64
                for t in range(2):
                    dst[at : at + 64, t * 128 : (t + 1) * 128] = jnp.where(
                        row == col + 2 * t, base, 0.0
                    ).astype(BF)
        cols = slice(half * 256, (half + 1) * 256)
        acc = jnp.zeros((tok, 128), F32)
        for p in range(PAIRS):
            acc = acc + f[:, p * 128 : (p + 1) * 128].astype(F32) * state[MAIN + p : MAIN + p + 1, :]
        high = acc.astype(BF)
        both = jnp.concatenate([high, (acc - high.astype(F32)).astype(BF)], axis=1)
        den = jnp.dot(both, span, preferred_element_type=F32) + den_ref[:, cols] + count
        at = MAIN + PAIRS
        vsum = jnp.concatenate([state[at : at + 1, :], state[at + 1 : at + 2, :]], axis=1)
        num = jnp.dot(f[...], dst[...], preferred_element_type=F32)
        o_ref[:, cols] = ((num + num_ref[:, cols] + vsum) / den).astype(BF)


SCALE = 1.0 / (math.sqrt(WDIM) * math.log(2.0))
QB = 2 * WINDOW


def masks():
    row, lane = rows_of((QB, QB)), lanes((QB, QB))
    earlier = (row < WINDOW) & (lane >= WINDOW)
    key = jnp.where(earlier, lane, lane + QB) - QB
    return earlier, key, (key <= row) & (key > row - WINDOW)


def attend(blocks, earlier, bias):
    s = jnp.stack(
        [
            lax.dot_general(q, k, (((1,), (1,)), ((), ())), preferred_element_type=F32)
            for q, k, v in blocks
        ]
    )
    s = jnp.where(earlier, s[:, :, :QB], s[:, :, QB:]) * SCALE + bias
    e = jnp.exp2(s - jnp.max(s, axis=2, keepdims=True))
    inverse = 1.0 / jnp.sum(e, axis=2, keepdims=True)
    e = jnp.concatenate([jnp.where(earlier, e, 0.0), jnp.where(earlier, 0.0, e)], axis=2).astype(BF)
    return [
        (jnp.dot(e[n], v, preferred_element_type=F32) * inverse[n]).astype(BF)
        for n, (q, k, v) in enumerate(blocks)
    ]


def window_kernel(q_ref, k_ref, v_ref, o_hbm, done, obuf, sems):
    done[...] = jnp.zeros_like(done)
    earlier, _, allowed = masks()
    bias = jnp.where(allowed, 0.0, -jnp.inf)
    tok, wide = q_ref.shape
    copies = []
    for h in range(0, wide, GROUP * WDIM):
        places = [
            (at, slice(c, c + WDIM))
            for c in range(h, h + GROUP * WDIM, WDIM)
            for at in range(QB, tok, QB)
        ]
        outs = attend(
            [
                (q_ref[at : at + QB, c], k_ref[at - QB : at + QB, c], v_ref[at - QB : at + QB, c])
                for at, c in places
            ],
            earlier,
            bias,
        )
        for (at, c), out in zip(places, outs):
            obuf[at : at + QB, c] = out
        part = (pl.ds(QB, tok - QB), pl.ds(h, GROUP * WDIM))
        copies.append(
            pltpu.make_async_copy(obuf.at[part], o_hbm.at[part], sems.at[h // (GROUP * WDIM)])
        )
        copies[-1].start()
    for copy in copies:
        copy.wait()


def edge_kernel(q_ref, k_ref, v_ref, h_ref, whole_ref, o_hbm, done, obuf, sems):
    done[...] = jnp.zeros_like(done)
    first = lax.axis_index("seq") == 0
    earlier, key, allowed = masks()
    bias = jnp.where(allowed & ((key >= 0) | jnp.logical_not(first)), 0.0, -jnp.inf)
    top = slice(0, QB)
    copies = []
    for h in range(0, q_ref.shape[1], 2 * GROUP * WDIM):
        blocks = []
        for c in range(h, h + 2 * GROUP * WDIM, WDIM):
            cols = slice(c, c + WDIM)
            kh, vh = h_ref[:WINDOW, cols], h_ref[WINDOW:, cols]
            k = jnp.concatenate([kh, kh, k_ref[top, cols]], axis=0)
            v = jnp.concatenate([vh, vh, v_ref[top, cols]], axis=0)
            blocks.append((q_ref[top, cols], k, v))
        for n, out in enumerate(attend(blocks, earlier, bias)):
            obuf[:, h + n * WDIM : h + (n + 1) * WDIM] = out
        part = (pl.ds(0, QB), pl.ds(h, 2 * GROUP * WDIM))
        copies.append(
            pltpu.make_async_copy(obuf.at[part], o_hbm.at[part], sems.at[h // (2 * GROUP * WDIM)])
        )
        copies[-1].start()
    for copy in copies:
        copy.wait()


def call(kernel, out, *args, in_specs, after=(), flops=0, nbytes=0, vmem=8, **kw):
    given = len(args)

    def run(*refs):
        kernel(*refs[:given], *refs[given + len(after) :])

    return pl.pallas_call(
        run,
        out_shape=out,
        in_specs=list(in_specs) + [pl.BlockSpec(memory_space=pl.ANY)] * len(after),
        cost_estimate=pl.CostEstimate(flops=flops, bytes_accessed=nbytes, transcendentals=0),
        compiler_params=pltpu.CompilerParams(vmem_limit_bytes=vmem << 20),
        name=kernel.__name__,
        **kw,
    )(*args, *after)


def exchange(x, step):
    count = lax.axis_size("seq")
    return lax.ppermute(x, "seq", [(i, i ^ step) for i in range(count)])


def shape(*dims, dtype=BF):
    return jax.ShapeDtypeStruct(dims, dtype)


def body(q_lin, k_lin, v_lin, q_win, k_win, v_win):
    tok = q_lin.shape[0]
    count = lax.axis_size("seq")
    assert count & (count - 1) == 0 and count > 1
    me = lax.axis_index("seq")
    bits = [(me & (1 << n)) != 0 for n in range(count.bit_length() - 1)]
    bits, k_lin = lax.optimization_barrier((bits, k_lin))
    wide = WHEADS * WDIM
    hbm = pl.BlockSpec(memory_space=pltpu.HBM)
    feats = pltpu.VMEM((tok, PAIRS * 128), BF)

    edge, q_lin, k_lin, v_lin = call(
        load_kernel,
        (
            shape(2 * WINDOW, wide),
            shape(*q_lin.shape),
            shape(*k_lin.shape),
            shape(*v_lin.shape),
        ),
        *(pltpu.with_memory_space_constraint(x, pltpu.HBM) for x in (q_lin, k_lin, v_lin, k_win, v_win)),
        in_specs=[hbm] * 5,
        out_specs=(VMEM,) * 4,
        scratch_shapes=[pltpu.SemaphoreType.DMA((5,))],
        nbytes=2 << 20,
        vmem=4,
    )
    edge = lax.ppermute(edge, "seq", [(i, (i + 1) % count) for i in range(count)])
    state = call(
        state_kernel,
        shape(2, ROWS, 128),
        k_lin,
        v_lin,
        in_specs=[VMEM] * 2,
        out_specs=VMEM,
        scratch_shapes=[feats] * 2,
        flops=1 << 30,
        nbytes=1 << 20,
    )
    peer = exchange(state, 1)
    both = state.astype(F32) + peer.astype(F32)
    carried = jnp.where(bits[0], both[1], both[0])
    before = jnp.zeros_like(carried)

    token = shape(8, 128, dtype=F32)

    def local(after):
        num, den, done = call(
            local_kernel,
            (shape(tok, HEADS * VDIM, dtype=F32),) * 2 + (token,),
            q_lin,
            k_lin,
            v_lin,
            after=after,
            in_specs=[VMEM] * 3,
            out_specs=(VMEM,) * 3,
            flops=1 << 31,
            nbytes=3 << 20,
        )
        return (num, den), (done,)

    def window(after):
        win, done = call(
            window_kernel,
            (shape(tok, wide), token),
            q_win,
            k_win,
            v_win,
            after=after,
            in_specs=[VMEM] * 3,
            out_specs=(hbm, VMEM),
            scratch_shapes=[
                pltpu.VMEM((tok, wide), BF),
                pltpu.SemaphoreType.DMA((WHEADS // GROUP,)),
            ],
            flops=1 << 31,
            nbytes=8 << 20,
        )
        return win, (done,)

    def rest(after, win):
        fa, fb, first = call(
            query_kernel,
            (shape(tok, PAIRS * 128),) * 2 + (token,),
            q_lin,
            after=after,
            in_specs=[VMEM],
            out_specs=(VMEM,) * 3,
            flops=1 << 28,
            nbytes=1 << 20,
        )
        out, second = call(
            edge_kernel,
            (shape(tok, wide), token),
            q_win,
            k_win,
            v_win,
            edge,
            win,
            after=after,
            in_specs=[VMEM] * 4 + [hbm],
            out_specs=(hbm, VMEM),
            scratch_shapes=[
                pltpu.VMEM((QB, wide), BF),
                pltpu.SemaphoreType.DMA((WHEADS // (2 * GROUP),)),
            ],
            input_output_aliases={4: 0},
            flops=1 << 28,
            nbytes=1 << 20,
        )
        return (fa, fb, out), (first, second)

    step, turn = 2, 0
    sums = win = feats = None
    done = ()
    while step < count:
        send = carried.astype(BF)
        got = exchange(send, step)
        after = (send,) + done
        if turn == 0:
            sums, done = local(after)
        elif turn == 1:
            win, done = window(after)
        elif turn == 2:
            feats, done = rest(after, win)
        if turn < 3:
            got, done = lax.optimization_barrier((got, done))
        got = got.astype(F32)
        before = before + jnp.where(bits[turn + 1], got, 0.0)
        carried = carried + got
        step *= 2
        turn += 1
    assert turn >= 3
    own = before.astype(BF)
    other = exchange(own, 1)
    lin_out = call(
        finish_kernel,
        shape(tok, HEADS * VDIM),
        *feats[:2],
        own,
        other,
        peer,
        *sums,
        after=done,
        in_specs=[VMEM] * 7,
        out_specs=VMEM,
        scratch_shapes=[pltpu.VMEM((PAIRS * 128, 256), BF)] * 2,
        flops=1 << 30,
        nbytes=3 << 20,
    )
    return (lin_out, feats[2])


def solution(mesh):
    spec = P(("groups", "seq"), None)
    return jax.shard_map(
        body, mesh=mesh, in_specs=(spec,) * 6, out_specs=(spec, spec), check_vma=False
    )
```

```python
import math

import jax
import jax.numpy as jnp
from jax import lax
from jax.experimental import pallas as pl
from jax.experimental.pallas import tpu as pltpu
from jax.sharding import PartitionSpec as P

HEADS = 8
KDIM = 16
VDIM = 64
WHEADS = 16
WDIM = 128
WINDOW = 64

BF = jnp.bfloat16
F32 = jnp.float32
BLOCKS = 10
PAIRS = BLOCKS // 2
MAIN = PAIRS * 64
ROWS = MAIN + 16
STEP = 256
GROUP = 4
COEF = (1 / 32,) + (1 / 16,) * 7 + (1 / 32, 1 / 4)
VMEM = pl.BlockSpec(memory_space=pltpu.VMEM)


def lanes(shape):
    return lax.broadcasted_iota(jnp.int32, shape, len(shape) - 1)


def rows_of(shape):
    return lax.broadcasted_iota(jnp.int32, shape, len(shape) - 2)


def feature(x, d):
    if d == 9:
        return x
    if d == 0:
        return x * x
    low = lanes(x.shape) % KDIM < KDIM - d
    other = jnp.where(low, pltpu.roll(x, 128 - d, 1), pltpu.roll(x, KDIM - d, 1))
    return x * other


def halves(first, second):
    left = lanes(first.shape) < 64
    return (
        jnp.where(left, first, pltpu.roll(second, 64, 1)),
        jnp.where(left, pltpu.roll(first, 64, 1), second),
    )


def put_features(x, coef, fa, fb):
    sums = []
    for p in range(PAIRS):
        blocks = [feature(x, d) * coef[d] for d in (2 * p, 2 * p + 1)]
        sums.append([jnp.sum(b, axis=0, keepdims=True) for b in blocks])
        a, b = halves(*blocks)
        fa[:, p * 128 : (p + 1) * 128] = a.astype(BF)
        fb[:, p * 128 : (p + 1) * 128] = b.astype(BF)
    return sums


def state_kernel(
    q_hbm, k_hbm, v_hbm, kw_hbm, vw_hbm, s_ref, ke_ref, ve_ref, q_ref, k_ref, v_ref, fa, fb, sems
):
    last = pl.ds(kw_hbm.shape[0] - WINDOW, WINDOW)
    moves = (
        (k_hbm, k_ref),
        (v_hbm, v_ref),
        (kw_hbm.at[last], ke_ref),
        (q_hbm, q_ref),
        (vw_hbm.at[last], ve_ref),
    )
    copies = [pltpu.make_async_copy(src, dst, sems.at[n]) for n, (src, dst) in enumerate(moves)]
    for copy in copies:
        copy.start()
    copies[0].wait()
    sums = put_features(k_ref[...].astype(F32), (1.0,) * BLOCKS, fa, fb)
    copies[1].wait()
    zs = [halves(*pair) for pair in sums]
    v = v_ref[...]
    vsum = jnp.sum(v.astype(F32), axis=0, keepdims=True)
    left = lanes((64, 128)) < 64
    even = (rows_of((64, 128)) // KDIM) % 2 == 0
    for half, f in ((0, fa), (1, fb)):
        r = lax.dot_general(
            f[...],
            v[:, half * 256 : (half + 1) * 256],
            (((0,), (0,)), ((), ())),
            preferred_element_type=F32,
        )
        for p in range(PAIRS):
            pieces = []
            for par in range(2):
                at = p * 128 + par * 64
                z = jnp.concatenate(
                    [r[at : at + 32, :128], r[at + 32 : at + 64, 128:]], axis=0
                )
                keep = even if par == 0 else jnp.logical_not(even)
                pieces.append(jnp.where(keep, z, pltpu.roll(z, 64, 1)))
            s_ref[half, p * 64 : (p + 1) * 64, :] = jnp.where(left, *pieces).astype(BF)
        aux = [z[half] for z in zs]
        aux += [vsum[:, half * 256 + t * 128 : half * 256 + (t + 1) * 128] for t in range(2)]
        aux.append(jnp.zeros((ROWS - MAIN - PAIRS - 2, 128), F32))
        s_ref[half, MAIN:, :] = jnp.concatenate(aux, axis=0).astype(BF)
    for copy in copies[2:]:
        copy.wait()


def local_kernel(q_ref, k_ref, v_ref, num_ref, den_ref, done):
    done[...] = jnp.zeros_like(done)
    tok = q_ref.shape[0]
    step = STEP
    k = k_ref[...]
    lane = lanes((step, 128))
    left = lane < 64
    left_all = lanes((tok, 128)) < 64
    causal = rows_of((step, step)) >= lanes((step, step))
    one = jnp.ones((tok, 128), BF)
    for r in range(tok // step):
        rows, end = slice(r * step, (r + 1) * step), (r + 1) * step
        q = q_ref[rows, :]
        for t0 in range(0, HEADS // 2, 2):
            places = [(t, e) for t in (t0, t0 + 1) for e in range(2)]
            kernels = []
            for t, e in places:
                qm = jnp.where(lane // KDIM == 2 * t + e, q, jnp.zeros_like(q))
                u = lax.dot_general(
                    qm, k[:end, :], (((1,), (1,)), ((), ())), preferred_element_type=F32
                )
                kernels.append(u + 4.0)
            outs = []
            for w, (t, e) in zip(kernels, places):
                w = w * w * (1 / 32) + 0.5
                diag = jnp.where(causal, w[:, r * step :], 0.0).astype(BF)
                if r:
                    diag = jnp.concatenate([w[:, : r * step].astype(BF), diag], axis=1)
                v = v_ref[:, t * 128 : (t + 1) * 128]
                aug = jnp.where(left_all, one, v) if e else jnp.where(left_all, v, one)
                outs.append(jnp.dot(diag, aug[:end, :], preferred_element_type=F32))
            for n in range(2):
                half, cols = t0 // 2, slice(n * 128, (n + 1) * 128)
                a, b = outs[2 * n : 2 * n + 2]
                num_ref[half, rows, cols] = jnp.where(left, a, b)
                den_ref[half, rows, cols] = pltpu.roll(jnp.where(left, b, a), 64, 1)


def finish_half(half, f_ref, e_ref, peer_ref, num_ref, den_ref, obuf, weights):
    tok = f_ref.shape[1]
    me = lax.axis_index("seq")
    core = me % 2
    left = lanes((64, 128)) < 64
    row = rows_of((64, 128)) // KDIM
    col = lanes((64, 128)) // VDIM
    span = ((rows_of((256, 256)) // KDIM) % 4 == lanes((256, 256)) // VDIM).astype(BF)
    count = (me * tok).astype(F32)
    state = e_ref[...].astype(F32) + jnp.where(core == 1, peer_ref[half].astype(F32), 0.0)
    for p in range(PAIRS):
        c = state[p * 64 : (p + 1) * 64, :]
        turned = pltpu.roll(c, 64, 1)
        for par in range(2):
            base = jnp.where(left, c, turned) if par == 0 else jnp.where(left, turned, c)
            at = p * 128 + par * 64
            for t in range(2):
                weights[at : at + 64, t * 128 : (t + 1) * 128] = jnp.where(
                    row == col + 2 * t, base, 0.0
                ).astype(BF)
    at = MAIN + PAIRS
    vsum = jnp.concatenate([state[at : at + 1, :], state[at + 1 : at + 2, :]], axis=1)
    step = tok // 2
    for n in range(2):
        rows = slice(n * step, (n + 1) * step)
        f = f_ref[half, rows, :]
        acc = jnp.zeros((step, 128), F32)
        for p in range(PAIRS):
            z = state[MAIN + p : MAIN + p + 1, :]
            acc = acc + f[:, p * 128 : (p + 1) * 128].astype(F32) * z
        high = acc.astype(BF)
        both = jnp.concatenate([high, (acc - high.astype(F32)).astype(BF)], axis=1)
        den = jnp.dot(both, span, preferred_element_type=F32) + den_ref[half, rows, :] + count
        num = jnp.dot(f, weights[...], preferred_element_type=F32)
        obuf[rows, :] = ((num + num_ref[half, rows, :] + vsum) / den).astype(BF)
        yield pl.ds(n * step, step)


SCALE = 1.0 / (math.sqrt(WDIM) * math.log(2.0))
QB = 2 * WINDOW


def masks():
    row, lane = rows_of((QB, QB)), lanes((QB, QB))
    earlier = (row < WINDOW) & (lane >= WINDOW)
    key = jnp.where(earlier, lane, lane + QB) - QB
    return earlier, (key <= row) & (key > row - WINDOW)


def attend(blocks, earlier, bias):
    s = jnp.stack(
        [
            lax.dot_general(q, k, (((1,), (1,)), ((), ())), preferred_element_type=F32)
            for q, k, v in blocks
        ]
    )
    s = jnp.where(earlier, s[:, :, :QB], s[:, :, QB:]) * SCALE + bias
    e = jnp.exp2(s - jnp.max(s, axis=2, keepdims=True))
    inverse = 1.0 / jnp.sum(e, axis=2, keepdims=True)
    e = jnp.concatenate([jnp.where(earlier, e, 0.0), jnp.where(earlier, 0.0, e)], axis=2).astype(BF)
    return [
        (jnp.dot(e[n], v, preferred_element_type=F32) * inverse[n]).astype(BF)
        for n, (q, k, v) in enumerate(blocks)
    ]


def window_kernel(q_ref, k_ref, v_ref, o_hbm, done, obuf, sems):
    done[...] = jnp.zeros_like(done)
    earlier, allowed = masks()
    bias = jnp.where(allowed, 0.0, -jnp.inf)
    tok, wide = q_ref.shape
    copies = []
    for h in range(0, wide, GROUP * WDIM):
        places = [
            (at, slice(c, c + WDIM))
            for c in range(h, h + GROUP * WDIM, WDIM)
            for at in range(QB, tok, QB)
        ]
        outs = attend(
            [
                (q_ref[at : at + QB, c], k_ref[at - QB : at + QB, c], v_ref[at - QB : at + QB, c])
                for at, c in places
            ],
            earlier,
            bias,
        )
        for (at, c), out in zip(places, outs):
            obuf[at : at + QB, c] = out
        part = (pl.ds(QB, tok - QB), pl.ds(h, GROUP * WDIM))
        copies.append(
            pltpu.make_async_copy(obuf.at[part], o_hbm.at[part], sems.at[h // (GROUP * WDIM)])
        )
        copies[-1].start()
    for copy in copies:
        copy.wait()


def narrow(q_ref, first_row, k_of, v_of, bias, o_hbm, obuf, sems):
    copies, group = [], 2 * GROUP * WDIM
    rows = slice(first_row, first_row + WINDOW)
    for h in range(0, q_ref.shape[1], group):
        places = [slice(c, c + WDIM) for c in range(h, h + group, WDIM)]
        s = jnp.stack(
            [
                lax.dot_general(
                    q_ref[rows, c], k_of(c), (((1,), (1,)), ((), ())), preferred_element_type=F32
                )
                for c in places
            ]
        )
        s = s * SCALE + bias
        e = jnp.exp2(s - jnp.max(s, axis=2, keepdims=True))
        inverse = 1.0 / jnp.sum(e, axis=2, keepdims=True)
        e = e.astype(BF)
        for n, c in enumerate(places):
            o = jnp.dot(e[n], v_of(c), preferred_element_type=F32) * inverse[n]
            obuf[:, c] = o.astype(BF)
        cols = pl.ds(h, group)
        copies.append(
            pltpu.make_async_copy(
                obuf.at[:, cols], o_hbm.at[pl.ds(first_row, WINDOW), cols], sems.at[h // group]
            )
        )
        copies[-1].start()
    return copies


def band():
    key, query = lanes((WINDOW, QB)), rows_of((WINDOW, QB))
    return (key > query) & (key <= query + WINDOW)


def query_kernel(x_ref, q_ref, k_ref, v_ref, whole_ref, f_ref, o_hbm, done, obuf, sems):
    done[...] = jnp.zeros_like(done)
    bias = jnp.where(band(), 0.0, -jnp.inf)
    copies = narrow(
        q_ref, WINDOW, lambda c: k_ref[:QB, c], lambda c: v_ref[:QB, c], bias, o_hbm, obuf, sems
    )
    put_features(x_ref[...].astype(F32), COEF, f_ref.at[0], f_ref.at[1])
    for copy in copies:
        copy.wait()


def own_kernel(f_ref, e_ref, peer_ref, num_ref, den_ref, o_ref, done, weights):
    done[...] = jnp.zeros_like(done)
    half = lax.axis_index("seq") % 2
    for rows in finish_half(half, f_ref, e_ref, peer_ref, num_ref, den_ref, o_ref, weights):
        pass


def tail_kernel(
    f_ref, e_ref, peer_ref, num_ref, den_ref, own_ref, q_ref, k_ref, v_ref, kh_ref, vh_ref,
    whole_ref, lin_hbm, win_hbm, weights, obuf, wbuf, lin_sems, win_sems,
):
    half = lax.axis_index("seq") % 2

    def put(ref, side, at, sem):
        copy = pltpu.make_async_copy(
            ref, lin_hbm.at[at, pl.ds(pl.multiple_of(side * 256, 256), 256)], sem
        )
        copy.start()
        return copy

    copies = [put(own_ref, half, pl.ds(0, f_ref.shape[1]), lin_sems.at[2])]
    for n, rows in enumerate(
        finish_half(1 - half, f_ref, e_ref, peer_ref, num_ref, den_ref, obuf, weights)
    ):
        copies.append(put(obuf.at[rows], 1 - half, rows, lin_sems.at[n]))
    allowed = band()
    follows = lax.axis_index("seq") > 0
    bias = jnp.where(allowed & ((lanes(allowed.shape) >= WINDOW) | follows), 0.0, -jnp.inf)

    def pair(edge, ref):
        return lambda c: jnp.concatenate([edge[:, c], ref[:WINDOW, c]], axis=0)

    copies += narrow(
        q_ref, 0, pair(kh_ref, k_ref), pair(vh_ref, v_ref), bias, win_hbm, wbuf, win_sems
    )
    for copy in copies:
        copy.wait()


def call(kernel, out, *args, in_specs, after=(), flops=0, nbytes=0, vmem=8, **kw):
    given = len(args)

    def run(*refs):
        kernel(*refs[:given], *refs[given + len(after) :])

    return pl.pallas_call(
        run,
        out_shape=out,
        in_specs=list(in_specs) + [pl.BlockSpec(memory_space=pl.ANY)] * len(after),
        cost_estimate=pl.CostEstimate(flops=flops, bytes_accessed=nbytes, transcendentals=0),
        compiler_params=pltpu.CompilerParams(vmem_limit_bytes=vmem << 20),
        name=kernel.__name__,
        **kw,
    )(*args, *after)


def exchange(x, step):
    count = lax.axis_size("seq")
    return lax.ppermute(x, "seq", [(i, i ^ step) for i in range(count)])


def shape(*dims, dtype=BF):
    return jax.ShapeDtypeStruct(dims, dtype)


def body(q_lin, k_lin, v_lin, q_win, k_win, v_win):
    tok = q_lin.shape[0]
    count = lax.axis_size("seq")
    assert count & (count - 1) == 0 and count > 1
    me = lax.axis_index("seq")
    bits = [(me & (1 << n)) != 0 for n in range(count.bit_length() - 1)]
    bits, k_lin = lax.optimization_barrier((bits, k_lin))
    wide = WHEADS * WDIM
    hbm = pl.BlockSpec(memory_space=pltpu.HBM)
    feats = pltpu.VMEM((tok, PAIRS * 128), BF)

    state, key_edge, val_edge, q_lin, k_lin, v_lin = call(
        state_kernel,
        (
            shape(2, ROWS, 128),
            shape(WINDOW, wide),
            shape(WINDOW, wide),
            shape(*q_lin.shape),
            shape(*k_lin.shape),
            shape(*v_lin.shape),
        ),
        *(pltpu.with_memory_space_constraint(x, pltpu.HBM) for x in (q_lin, k_lin, v_lin, k_win, v_win)),
        in_specs=[hbm] * 5,
        out_specs=(VMEM,) * 6,
        scratch_shapes=[feats] * 2 + [pltpu.SemaphoreType.DMA((5,))],
        flops=1 << 30,
        nbytes=2 << 20,
    )

    def ring(x, after):
        x, after = lax.optimization_barrier((x, after))
        return lax.ppermute(x, "seq", [(i, (i + 1) % count) for i in range(count)]), after

    peer = exchange(state, 1)
    both = state.astype(F32) + peer.astype(F32)
    carried = jnp.where(bits[0], both[1], both[0])
    before = jnp.zeros_like(carried)

    token = shape(8, 128, dtype=F32)

    def local(after):
        num, den, done = call(
            local_kernel,
            (shape(2, tok, HEADS * VDIM // 2, dtype=F32),) * 2 + (token,),
            q_lin,
            k_lin,
            v_lin,
            after=after,
            in_specs=[VMEM] * 3,
            out_specs=(VMEM,) * 3,
            flops=1 << 31,
            nbytes=3 << 20,
        )
        return (num, den), (done,)

    def window(after):
        win, done = call(
            window_kernel,
            (shape(tok, wide), token),
            q_win,
            k_win,
            v_win,
            after=after,
            in_specs=[VMEM] * 3,
            out_specs=(hbm, VMEM),
            scratch_shapes=[
                pltpu.VMEM((tok, wide), BF),
                pltpu.SemaphoreType.DMA((WHEADS // GROUP,)),
            ],
            flops=1 << 31,
            nbytes=8 << 20,
        )
        return win, (done,)

    def query(after, win):
        feats, win, done = call(
            query_kernel,
            (shape(2, tok, PAIRS * 128), shape(tok, wide), token),
            q_lin,
            q_win,
            k_win,
            v_win,
            win,
            after=after,
            in_specs=[VMEM] * 4 + [hbm],
            out_specs=(VMEM, hbm, VMEM),
            scratch_shapes=[
                pltpu.VMEM((WINDOW, wide), BF),
                pltpu.SemaphoreType.DMA((WHEADS // (2 * GROUP),)),
            ],
            input_output_aliases={4: 1},
            flops=1 << 29,
            nbytes=2 << 20,
        )
        return feats, win, (done,)

    step, turn = 2, 0
    sums = win = feats = None
    done = ()
    while step < count:
        send = carried.astype(BF)
        if turn == 0:
            key_edge, send = ring(key_edge, send)
        elif turn == 1:
            val_edge, send = ring(val_edge, send)
        got = exchange(send, step)
        after = (send,) + done
        if turn == 0:
            sums, done = local(after)
        elif turn == 1:
            win, done = window(after)
        elif turn == 2:
            feats, win, done = query(after, win)
        if turn == 2:
            got, done, key_edge, val_edge = lax.optimization_barrier((got, done, key_edge, val_edge))
        elif turn < 2:
            got, done = lax.optimization_barrier((got, done))
        got = got.astype(F32)
        before = before + jnp.where(bits[turn + 1], got, 0.0)
        carried = carried + got
        step *= 2
        turn += 1
    assert turn >= 3
    own = before.astype(BF)
    other = exchange(own, 1)
    weights = pltpu.VMEM((PAIRS * 128, 256), BF)
    mine, last = call(
        own_kernel,
        (shape(tok, HEADS * VDIM // 2), token),
        feats,
        own,
        peer,
        *sums,
        after=done,
        in_specs=[VMEM] * 5,
        out_specs=(VMEM, VMEM),
        scratch_shapes=[weights],
        flops=1 << 29,
        nbytes=2 << 20,
    )
    other, last = lax.optimization_barrier((other, last))
    return call(
        tail_kernel,
        (shape(tok, HEADS * VDIM), shape(tok, wide)),
        feats,
        other,
        peer,
        *sums,
        mine,
        q_win,
        k_win,
        v_win,
        key_edge,
        val_edge,
        win,
        after=(last,),
        in_specs=[VMEM] * 11 + [hbm],
        out_specs=(hbm, hbm),
        scratch_shapes=[
            weights,
            pltpu.VMEM((tok, HEADS * VDIM // 2), BF),
            pltpu.VMEM((WINDOW, wide), BF),
            pltpu.SemaphoreType.DMA((3,)),
            pltpu.SemaphoreType.DMA((WHEADS // (2 * GROUP),)),
        ],
        input_output_aliases={11: 1},
        flops=1 << 29,
        nbytes=3 << 20,
    )


def solution(mesh):
    spec = P(("groups", "seq"), None)
    return jax.shard_map(
        body, mesh=mesh, in_specs=(spec,) * 6, out_specs=(spec, spec), check_vma=False
    )
```

```python
import math

import jax
import jax.numpy as jnp
from jax import lax
from jax.experimental import pallas as pl
from jax.experimental.pallas import tpu as pltpu
from jax.sharding import PartitionSpec as P

HEADS = 8
KDIM = 16
VDIM = 64
WHEADS = 16
WDIM = 128
WINDOW = 64

BF = jnp.bfloat16
F32 = jnp.float32
BLOCKS = 10
PAIRS = BLOCKS // 2
MAIN = PAIRS * 64
ROWS = MAIN + 16
STEP = 256
GROUP = 4
COEF = (1 / 32,) + (1 / 16,) * 7 + (1 / 32, 1 / 4)
VMEM = pl.BlockSpec(memory_space=pltpu.VMEM)


def lanes(shape):
    return lax.broadcasted_iota(jnp.int32, shape, len(shape) - 1)


def rows_of(shape):
    return lax.broadcasted_iota(jnp.int32, shape, len(shape) - 2)


def feature_pairs(x, coef):
    src, dst = rows_of((128, 256)), lanes((128, 256))
    order = (src // KDIM == dst // 128 * 4 + dst % 4) & (src % KDIM == dst % 64 // 4)
    y = jnp.dot(x, order.astype(BF), preferred_element_type=F32)
    left = lanes((x.shape[0], 128)) < 64
    for p in range(PAIRS):
        pair = []
        for half in range(2):
            own = y[:, half * 128 : (half + 1) * 128]
            others = []
            for d in (2 * p, 2 * p + 1):
                if d == 9:
                    others.append(jnp.ones_like(own))
                else:
                    others.append(pltpu.roll(own, 128 - 4 * d, 1) if d else own)
            f = own * jnp.where(left, *others)
            if coef is not None:
                low, high = coef[2 * p : 2 * p + 2]
                f = f * (low if low == high else jnp.where(left, low, high))
            pair.append(f)
        yield pair


def state_kernel(
    q_hbm, k_hbm, v_hbm, kw_hbm, vw_hbm, s_ref, ke_ref, ve_ref, q_ref, k_ref, v_ref, f_ref, sems
):
    last = pl.ds(kw_hbm.shape[0] - WINDOW, WINDOW)
    moves = (
        (k_hbm, k_ref),
        (v_hbm, v_ref),
        (kw_hbm.at[last], ke_ref),
        (q_hbm, q_ref),
        (vw_hbm.at[last], ve_ref),
    )
    copies = [pltpu.make_async_copy(src, dst, sems.at[n]) for n, (src, dst) in enumerate(moves)]
    for copy in copies:
        copy.start()
    copies[0].wait()
    sums = []
    for p, pair in enumerate(feature_pairs(k_ref[...], None)):
        sums.append([jnp.sum(f, axis=0, keepdims=True) for f in pair])
        for half, f in enumerate(pair):
            f_ref[half, :, p * 128 : (p + 1) * 128] = f.astype(BF)
    copies[1].wait()
    v = v_ref[...]
    vsum = jnp.sum(v.astype(F32), axis=0, keepdims=True)
    left = lanes((64, 128)) < 64
    head = rows_of((64, 128)) % 4
    for half in range(2):
        r = lax.dot_general(
            f_ref[half],
            v[:, half * 256 : (half + 1) * 256],
            (((0,), (0,)), ((), ())),
            preferred_element_type=F32,
        )
        for p in range(PAIRS):
            pieces = []
            for par in range(2):
                at = p * 128 + par * 64
                z = jnp.where(head < 2, r[at : at + 64, :128], r[at : at + 64, 128:])
                pieces.append(jnp.where(head % 2 == par, z, pltpu.roll(z, 64, 1)))
            s_ref[half, p * 64 : (p + 1) * 64, :] = jnp.where(left, *pieces).astype(BF)
        aux = [total[half] for total in sums]
        aux += [vsum[:, half * 256 + t * 128 : half * 256 + (t + 1) * 128] for t in range(2)]
        aux.append(jnp.zeros((ROWS - MAIN - PAIRS - 2, 128), F32))
        s_ref[half, MAIN:, :] = jnp.concatenate(aux, axis=0).astype(BF)
    for copy in copies[2:]:
        copy.wait()


def local_kernel(q_ref, k_ref, v_ref, num_ref, den_ref, done):
    done[...] = jnp.zeros_like(done)
    tok = q_ref.shape[0]
    step = STEP
    k = k_ref[...]
    lane = lanes((step, 128))
    left = lane < 64
    left_all = lanes((tok, 128)) < 64
    causal = rows_of((step, step)) >= lanes((step, step))
    one = jnp.ones((tok, 128), BF)
    for r in range(tok // step):
        rows, end = slice(r * step, (r + 1) * step), (r + 1) * step
        q = q_ref[rows, :]
        for t0 in range(0, HEADS // 2, 2):
            places = [(t, e) for t in (t0, t0 + 1) for e in range(2)]
            kernels = []
            for t, e in places:
                qm = jnp.where(lane // KDIM == 2 * t + e, q, jnp.zeros_like(q))
                u = lax.dot_general(
                    qm, k[:end, :], (((1,), (1,)), ((), ())), preferred_element_type=F32
                )
                kernels.append(u + 4.0)
            outs = []
            for w, (t, e) in zip(kernels, places):
                w = w * w * (1 / 32) + 0.5
                diag = jnp.where(causal, w[:, r * step :], 0.0).astype(BF)
                if r:
                    diag = jnp.concatenate([w[:, : r * step].astype(BF), diag], axis=1)
                v = v_ref[:, t * 128 : (t + 1) * 128]
                aug = jnp.where(left_all, one, v) if e else jnp.where(left_all, v, one)
                outs.append(jnp.dot(diag, aug[:end, :], preferred_element_type=F32))
            for n in range(2):
                half, cols = t0 // 2, slice(n * 128, (n + 1) * 128)
                a, b = outs[2 * n : 2 * n + 2]
                num_ref[half, rows, cols] = jnp.where(left, a, b)
                den_ref[half, rows, cols] = pltpu.roll(jnp.where(left, b, a), 64, 1)


def finish_half(half, f_ref, e_ref, peer_ref, num_ref, den_ref, obuf, weights):
    tok = f_ref.shape[1]
    me = lax.axis_index("seq")
    core = me % 2
    left = lanes((64, 128)) < 64
    row = rows_of((64, 128)) % 4
    col = lanes((64, 128)) // VDIM
    span = (rows_of((256, 256)) % 4 == lanes((256, 256)) // VDIM).astype(BF)
    count = (me * tok).astype(F32)
    state = e_ref[...].astype(F32) + jnp.where(core == 1, peer_ref[half].astype(F32), 0.0)
    for p in range(PAIRS):
        c = state[p * 64 : (p + 1) * 64, :]
        turned = pltpu.roll(c, 64, 1)
        for par in range(2):
            base = jnp.where(left, c, turned) if par == 0 else jnp.where(left, turned, c)
            at = p * 128 + par * 64
            for t in range(2):
                weights[at : at + 64, t * 128 : (t + 1) * 128] = jnp.where(
                    row == col + 2 * t, base, 0.0
                ).astype(BF)
    at = MAIN + PAIRS
    vsum = jnp.concatenate([state[at : at + 1, :], state[at + 1 : at + 2, :]], axis=1)
    step = tok // 2
    for n in range(2):
        rows = slice(n * step, (n + 1) * step)
        f = f_ref[half, rows, :]
        acc = jnp.zeros((step, 128), F32)
        for p in range(PAIRS):
            z = state[MAIN + p : MAIN + p + 1, :]
            acc = acc + f[:, p * 128 : (p + 1) * 128].astype(F32) * z
        high = acc.astype(BF)
        both = jnp.concatenate([high, (acc - high.astype(F32)).astype(BF)], axis=1)
        den = jnp.dot(both, span, preferred_element_type=F32) + den_ref[half, rows, :] + count
        num = jnp.dot(f, weights[...], preferred_element_type=F32)
        obuf[rows, :] = ((num + num_ref[half, rows, :] + vsum) / den).astype(BF)
        yield pl.ds(n * step, step)


SCALE = 1.0 / (math.sqrt(WDIM) * math.log(2.0))
QB = 2 * WINDOW


def masks():
    row, lane = rows_of((QB, QB)), lanes((QB, QB))
    earlier = (row < WINDOW) & (lane >= WINDOW)
    key = jnp.where(earlier, lane, lane + QB) - QB
    return earlier, (key <= row) & (key > row - WINDOW)


def attend(blocks, earlier, bias):
    s = jnp.stack(
        [
            lax.dot_general(q, k, (((1,), (1,)), ((), ())), preferred_element_type=F32)
            for q, k, v in blocks
        ]
    )
    s = jnp.where(earlier, s[:, :, :QB], s[:, :, QB:]) * SCALE + bias
    e = jnp.exp2(s - jnp.max(s, axis=2, keepdims=True))
    inverse = 1.0 / jnp.sum(e, axis=2, keepdims=True)
    e = jnp.concatenate([jnp.where(earlier, e, 0.0), jnp.where(earlier, 0.0, e)], axis=2).astype(BF)
    return [
        (jnp.dot(e[n], v, preferred_element_type=F32) * inverse[n]).astype(BF)
        for n, (q, k, v) in enumerate(blocks)
    ]


def window_kernel(q_ref, k_ref, v_ref, o_hbm, done, obuf, sems):
    done[...] = jnp.zeros_like(done)
    earlier, allowed = masks()
    bias = jnp.where(allowed, 0.0, -jnp.inf)
    tok, wide = q_ref.shape
    copies = []
    for h in range(0, wide, GROUP * WDIM):
        places = [
            (at, slice(c, c + WDIM))
            for c in range(h, h + GROUP * WDIM, WDIM)
            for at in range(QB, tok, QB)
        ]
        outs = attend(
            [
                (q_ref[at : at + QB, c], k_ref[at - QB : at + QB, c], v_ref[at - QB : at + QB, c])
                for at, c in places
            ],
            earlier,
            bias,
        )
        for (at, c), out in zip(places, outs):
            obuf[at : at + QB, c] = out
        part = (pl.ds(QB, tok - QB), pl.ds(h, GROUP * WDIM))
        copies.append(
            pltpu.make_async_copy(obuf.at[part], o_hbm.at[part], sems.at[h // (GROUP * WDIM)])
        )
        copies[-1].start()
    for copy in copies:
        copy.wait()


def narrow_weights(q_ref, first_row, k_of, bias, put):
    group = 2 * GROUP * WDIM
    rows = slice(first_row, first_row + WINDOW)
    for h in range(0, q_ref.shape[1], group):
        places = [slice(c, c + WDIM) for c in range(h, h + group, WDIM)]
        s = jnp.stack(
            [
                lax.dot_general(
                    q_ref[rows, c], k_of(c), (((1,), (1,)), ((), ())), preferred_element_type=F32
                )
                for c in places
            ]
        )
        s = s * SCALE + bias
        e = jnp.exp2(s - jnp.max(s, axis=2, keepdims=True))
        e = (e * (1.0 / jnp.sum(e, axis=2, keepdims=True))).astype(BF)
        for n, c in enumerate(places):
            put(c, e[n])


def band():
    key, query = lanes((WINDOW, QB)), rows_of((WINDOW, QB))
    return (key > query) & (key <= query + WINDOW)


def query_kernel(x_ref, f_ref, done):
    done[...] = jnp.zeros_like(done)
    for p, pair in enumerate(feature_pairs(x_ref[...], COEF)):
        for half, f in enumerate(pair):
            f_ref[half, :, p * 128 : (p + 1) * 128] = f.astype(BF)


def top_kernel(q_ref, k_ref, v_ref, kh_ref, whole_ref, w_ref, o_hbm, done, obuf, sem):
    done[...] = jnp.zeros_like(done)
    allowed = band()

    def put(c, w):
        obuf[:, c] = jnp.dot(w, v_ref[:QB, c], preferred_element_type=F32).astype(BF)

    narrow_weights(
        q_ref, WINDOW, lambda c: k_ref[:QB, c], jnp.where(allowed, 0.0, -jnp.inf), put
    )
    copy = pltpu.make_async_copy(obuf, o_hbm.at[pl.ds(WINDOW, WINDOW)], sem)
    copy.start()
    follows = lax.axis_index("seq") > 0
    bias = jnp.where(allowed & ((lanes(allowed.shape) >= WINDOW) | follows), 0.0, -jnp.inf)

    def keep(c, w):
        w_ref[:, c] = w

    narrow_weights(
        q_ref, 0, lambda c: jnp.concatenate([kh_ref[:, c], k_ref[:WINDOW, c]], axis=0), bias, keep
    )
    copy.wait()


def own_kernel(
    f_ref, e_ref, peer_ref, num_ref, den_ref, w_ref, v_ref, vh_ref, o_ref, top_ref, weights
):
    half = lax.axis_index("seq") % 2
    for rows in finish_half(half, f_ref, e_ref, peer_ref, num_ref, den_ref, o_ref, weights):
        pass
    for c in range(0, w_ref.shape[1], WDIM):
        c = slice(c, c + WDIM)
        v = jnp.concatenate([vh_ref[:, c], v_ref[:WINDOW, c]], axis=0)
        top_ref[:, c] = jnp.dot(w_ref[:, c], v, preferred_element_type=F32).astype(BF)


def tail_kernel(
    f_ref, e_ref, peer_ref, num_ref, den_ref, own_ref, top_ref, whole_ref,
    lin_hbm, win_hbm, weights, obuf, sems,
):
    half = lax.axis_index("seq") % 2

    def put(ref, side, at, sem):
        copy = pltpu.make_async_copy(
            ref, lin_hbm.at[at, pl.ds(pl.multiple_of(side * 256, 256), 256)], sem
        )
        copy.start()
        return copy

    copies = [
        pltpu.make_async_copy(top_ref, win_hbm.at[pl.ds(0, WINDOW)], sems.at[3]),
        put(own_ref, half, pl.ds(0, f_ref.shape[1]), sems.at[2]),
    ]
    copies[0].start()
    for n, rows in enumerate(
        finish_half(1 - half, f_ref, e_ref, peer_ref, num_ref, den_ref, obuf, weights)
    ):
        copies.append(put(obuf.at[rows], 1 - half, rows, sems.at[n]))
    for copy in copies:
        copy.wait()


def call(kernel, out, *args, in_specs, after=(), flops=0, nbytes=0, vmem=8, **kw):
    given = len(args)

    def run(*refs):
        kernel(*refs[:given], *refs[given + len(after) :])

    return pl.pallas_call(
        run,
        out_shape=out,
        in_specs=list(in_specs) + [pl.BlockSpec(memory_space=pl.ANY)] * len(after),
        cost_estimate=pl.CostEstimate(flops=flops, bytes_accessed=nbytes, transcendentals=0),
        compiler_params=pltpu.CompilerParams(vmem_limit_bytes=vmem << 20),
        name=kernel.__name__,
        **kw,
    )(*args, *after)


def exchange(x, step):
    count = lax.axis_size("seq")
    return lax.ppermute(x, "seq", [(i, i ^ step) for i in range(count)])


def shape(*dims, dtype=BF):
    return jax.ShapeDtypeStruct(dims, dtype)


def body(q_lin, k_lin, v_lin, q_win, k_win, v_win):
    tok = q_lin.shape[0]
    count = lax.axis_size("seq")
    assert count & (count - 1) == 0 and count > 1
    me = lax.axis_index("seq")
    bits = [(me & (1 << n)) != 0 for n in range(count.bit_length() - 1)]
    bits, k_lin = lax.optimization_barrier((bits, k_lin))
    wide = WHEADS * WDIM
    hbm = pl.BlockSpec(memory_space=pltpu.HBM)

    state, key_edge, val_edge, q_lin, k_lin, v_lin = call(
        state_kernel,
        (
            shape(2, ROWS, 128),
            shape(WINDOW, wide),
            shape(WINDOW, wide),
            shape(*q_lin.shape),
            shape(*k_lin.shape),
            shape(*v_lin.shape),
        ),
        *(pltpu.with_memory_space_constraint(x, pltpu.HBM) for x in (q_lin, k_lin, v_lin, k_win, v_win)),
        in_specs=[hbm] * 5,
        out_specs=(VMEM,) * 6,
        scratch_shapes=[pltpu.VMEM((2, tok, PAIRS * 128), BF), pltpu.SemaphoreType.DMA((5,))],
        flops=1 << 30,
        nbytes=2 << 20,
    )

    def ring(x, after):
        x, after = lax.optimization_barrier((x, after))
        return lax.ppermute(x, "seq", [(i, (i + 1) % count) for i in range(count)]), after

    peer = exchange(state, 1)
    token = shape(8, 128, dtype=F32)
    feats, first = call(
        query_kernel,
        (shape(2, tok, PAIRS * 128), token),
        q_lin,
        after=(state,),
        in_specs=[VMEM],
        out_specs=(VMEM, VMEM),
        flops=1 << 28,
        nbytes=2 << 20,
    )
    done = (first,)
    peer, done = lax.optimization_barrier((peer, done))
    both = state.astype(F32) + peer.astype(F32)
    carried = jnp.where(bits[0], both[1], both[0])
    before = jnp.zeros_like(carried)

    def local(after):
        num, den, done = call(
            local_kernel,
            (shape(2, tok, HEADS * VDIM // 2, dtype=F32),) * 2 + (token,),
            q_lin,
            k_lin,
            v_lin,
            after=after,
            in_specs=[VMEM] * 3,
            out_specs=(VMEM,) * 3,
            flops=1 << 31,
            nbytes=3 << 20,
        )
        return (num, den), (done,)

    def window(after):
        win, done = call(
            window_kernel,
            (shape(tok, wide), token),
            q_win,
            k_win,
            v_win,
            after=after,
            in_specs=[VMEM] * 3,
            out_specs=(hbm, VMEM),
            scratch_shapes=[
                pltpu.VMEM((tok, wide), BF),
                pltpu.SemaphoreType.DMA((WHEADS // GROUP,)),
            ],
            flops=1 << 31,
            nbytes=8 << 20,
        )
        return win, (done,)

    def top(after, win):
        shares, win, done = call(
            top_kernel,
            (shape(WINDOW, wide), shape(tok, wide), token),
            q_win,
            k_win,
            v_win,
            key_edge,
            win,
            after=after,
            in_specs=[VMEM] * 4 + [hbm],
            out_specs=(VMEM, hbm, VMEM),
            scratch_shapes=[pltpu.VMEM((WINDOW, wide), BF), pltpu.SemaphoreType.DMA],
            input_output_aliases={4: 1},
            flops=1 << 30,
            nbytes=2 << 20,
        )
        return shares, win, (done,)

    step, turn = 2, 0
    sums = win = shares = None
    while step < count:
        send = carried.astype(BF)
        if turn == 0:
            key_edge, send = ring(key_edge, send)
        elif turn == 1:
            val_edge, send = ring(val_edge, send)
        got = exchange(send, step + step // 2 if 2 * step == count else step)
        after = (send,) + done
        if turn == 0:
            sums, done = local(after)
        elif turn == 1:
            win, done = window(after)
        elif turn == 2:
            shares, win, done = top(after, win)
        if turn == 2:
            got, done, val_edge = lax.optimization_barrier((got, done, val_edge))
        elif turn < 2:
            got, done = lax.optimization_barrier((got, done))
        got = got.astype(F32)
        before = before + jnp.where(bits[turn + 1], got, 0.0)
        carried = carried + got
        step *= 2
        turn += 1
    assert turn >= 3
    own = before.astype(BF)
    other = exchange(own, 1)
    weights = pltpu.VMEM((PAIRS * 128, 256), BF)
    mine, top = call(
        own_kernel,
        (shape(tok, HEADS * VDIM // 2), shape(WINDOW, wide)),
        feats,
        own,
        peer,
        *sums,
        shares,
        v_win,
        val_edge,
        after=done,
        in_specs=[VMEM] * 8,
        out_specs=(VMEM, VMEM),
        scratch_shapes=[weights],
        flops=1 << 30,
        nbytes=3 << 20,
    )
    other, mine, top = lax.optimization_barrier((other, mine, top))
    return call(
        tail_kernel,
        (shape(tok, HEADS * VDIM), shape(tok, wide)),
        feats,
        other,
        peer,
        *sums,
        mine,
        top,
        win,
        in_specs=[VMEM] * 7 + [hbm],
        out_specs=(hbm, hbm),
        scratch_shapes=[
            weights,
            pltpu.VMEM((tok, HEADS * VDIM // 2), BF),
            pltpu.SemaphoreType.DMA((4,)),
        ],
        input_output_aliases={7: 1},
        flops=1 << 29,
        nbytes=2 << 20,
    )


def solution(mesh):
    spec = P(("groups", "seq"), None)
    return jax.shard_map(
        body, mesh=mesh, in_specs=(spec,) * 6, out_specs=(spec, spec), check_vma=False
    )
```

```python
import math

import jax
import jax.numpy as jnp
from jax import lax
from jax.experimental import pallas as pl
from jax.experimental.pallas import tpu as pltpu
from jax.sharding import PartitionSpec as P

HEADS = 8
KDIM = 16
VDIM = 64
WHEADS = 16
WDIM = 128
WINDOW = 64

BF = jnp.bfloat16
F32 = jnp.float32
BLOCKS = 10
PAIRS = BLOCKS // 2
MAIN = PAIRS * 64
ROWS = MAIN + 16
STEP = 256
GROUP = 4
COEF = (1 / 32,) + (1 / 16,) * 7 + (1 / 32, 1 / 4)
VMEM = pl.BlockSpec(memory_space=pltpu.VMEM)


def lanes(shape):
    return lax.broadcasted_iota(jnp.int32, shape, len(shape) - 1)


def rows_of(shape):
    return lax.broadcasted_iota(jnp.int32, shape, len(shape) - 2)


def orders():
    dims = (128, (1 + PAIRS) * 256)
    src, dst = rows_of(dims), lanes(dims)
    d = jnp.where(dst < 256, 0, dst // 256 * 2 - 2 + dst % 128 // 64)
    head, entry = dst % 256 // 128 * 4 + dst % 4, (dst % 64 // 4 + d) % KDIM
    return (src == head * KDIM + entry).astype(BF)


def feature_pairs(x, order, coef):
    own = jnp.dot(x, order[:, :256], preferred_element_type=F32)
    others = jnp.dot(x, order[:, 256:], preferred_element_type=F32)
    left = lanes((x.shape[0], 128)) < 64
    for p in range(PAIRS):
        pair = []
        for half in range(2):
            at = p * 256 + half * 128
            other = others[:, at : at + 128]
            if p == PAIRS - 1:
                other = jnp.where(left, other, 1.0)
            f = own[:, half * 128 : (half + 1) * 128] * other
            if coef is not None:
                low, high = coef[2 * p : 2 * p + 2]
                f = f * (low if low == high else jnp.where(left[:1], low, high))
            pair.append(f)
        yield pair


def state_kernel(
    q_hbm, k_hbm, v_hbm, kw_hbm, vw_hbm,
    s_ref, ke_ref, ve_ref, q_ref, k_ref, v_ref, order_ref, f_ref, sems,
):
    last = pl.ds(kw_hbm.shape[0] - WINDOW, WINDOW)
    moves = (
        (k_hbm, k_ref),
        (v_hbm, v_ref),
        (kw_hbm.at[last], ke_ref),
        (q_hbm, q_ref),
        (vw_hbm.at[last], ve_ref),
    )
    copies = [pltpu.make_async_copy(src, dst, sems.at[n]) for n, (src, dst) in enumerate(moves)]
    for copy in copies:
        copy.start()
    order_ref[...] = orders()
    copies[0].wait()
    sums = []
    for p, pair in enumerate(feature_pairs(k_ref[...], order_ref[...], None)):
        sums.append([jnp.sum(f, axis=0, keepdims=True) for f in pair])
        for half, f in enumerate(pair):
            f_ref[half, :, p * 128 : (p + 1) * 128] = f.astype(BF)
    copies[1].wait()
    v = v_ref[...]
    vsum = jnp.sum(v.astype(F32), axis=0, keepdims=True)
    left = lanes((64, 128)) < 64
    head = rows_of((64, 128)) % 4
    for half in range(2):
        r = lax.dot_general(
            f_ref[half],
            v[:, half * 256 : (half + 1) * 256],
            (((0,), (0,)), ((), ())),
            preferred_element_type=F32,
        )
        for p in range(PAIRS):
            pieces = []
            for par in range(2):
                at = p * 128 + par * 64
                z = jnp.where(head < 2, r[at : at + 64, :128], r[at : at + 64, 128:])
                pieces.append(jnp.where(head % 2 == par, z, pltpu.roll(z, 64, 1)))
            s_ref[half, p * 64 : (p + 1) * 64, :] = jnp.where(left, *pieces).astype(BF)
        aux = [total[half] for total in sums]
        aux += [vsum[:, half * 256 + t * 128 : half * 256 + (t + 1) * 128] for t in range(2)]
        aux.append(jnp.zeros((ROWS - MAIN - PAIRS - 2, 128), F32))
        s_ref[half, MAIN:, :] = jnp.concatenate(aux, axis=0).astype(BF)
    for copy in copies[2:]:
        copy.wait()


def local_kernel(q_ref, k_ref, v_ref, num_ref, den_ref, done):
    done[...] = jnp.zeros_like(done)
    tok = q_ref.shape[0]
    step = STEP
    k = k_ref[...]
    lane = lanes((step, 128))
    left = lane < 64
    left_all = lanes((tok, 128)) < 64
    causal = rows_of((step, step)) >= lanes((step, step))
    one = jnp.ones((tok, 128), BF)
    for r in range(tok // step):
        rows, end = slice(r * step, (r + 1) * step), (r + 1) * step
        q = q_ref[rows, :]
        for t0 in range(0, HEADS // 2, 2):
            places = [(t, e) for t in (t0, t0 + 1) for e in range(2)]
            kernels = []
            for t, e in places:
                qm = jnp.where(lane // KDIM == 2 * t + e, q, jnp.zeros_like(q))
                u = lax.dot_general(
                    qm, k[:end, :], (((1,), (1,)), ((), ())), preferred_element_type=F32
                )
                kernels.append(u + 4.0)
            outs = []
            for w, (t, e) in zip(kernels, places):
                w = w * w * (1 / 32) + 0.5
                diag = jnp.where(causal, w[:, r * step :], 0.0).astype(BF)
                if r:
                    diag = jnp.concatenate([w[:, : r * step].astype(BF), diag], axis=1)
                v = v_ref[:, t * 128 : (t + 1) * 128]
                aug = jnp.where(left_all, one, v) if e else jnp.where(left_all, v, one)
                outs.append(jnp.dot(diag, aug[:end, :], preferred_element_type=F32))
            for n in range(2):
                half, cols = t0 // 2, slice(n * 128, (n + 1) * 128)
                a, b = outs[2 * n : 2 * n + 2]
                num_ref[half, rows, cols] = jnp.where(left, a, b)
                den_ref[half, rows, cols] = pltpu.roll(jnp.where(left, b, a), 64, 1)


def finish_half(half, f_ref, e_ref, peer_ref, num_ref, den_ref, obuf, weights):
    tok = f_ref.shape[1]
    me = lax.axis_index("seq")
    core = me % 2
    left = lanes((64, 128)) < 64
    row = rows_of((64, 128)) % 4
    col = lanes((64, 128)) // VDIM
    span = (rows_of((256, 256)) % 4 == lanes((256, 256)) // VDIM).astype(BF)
    count = (me * tok).astype(F32)
    state = e_ref[...].astype(F32) + jnp.where(core == 1, peer_ref[half].astype(F32), 0.0)
    for p in range(PAIRS):
        c = state[p * 64 : (p + 1) * 64, :]
        turned = pltpu.roll(c, 64, 1)
        for par in range(2):
            base = jnp.where(left, c, turned) if par == 0 else jnp.where(left, turned, c)
            at = p * 128 + par * 64
            for t in range(2):
                weights[at : at + 64, t * 128 : (t + 1) * 128] = jnp.where(
                    row == col + 2 * t, base, 0.0
                ).astype(BF)
    at = MAIN + PAIRS
    vsum = jnp.concatenate([state[at : at + 1, :], state[at + 1 : at + 2, :]], axis=1)
    step = tok // 4
    for n in range(tok // step):
        rows = slice(n * step, (n + 1) * step)
        f = f_ref[half, rows, :]
        acc = jnp.zeros((step, 128), F32)
        for p in range(PAIRS):
            z = state[MAIN + p : MAIN + p + 1, :]
            acc = acc + f[:, p * 128 : (p + 1) * 128].astype(F32) * z
        high = acc.astype(BF)
        both = jnp.concatenate([high, (acc - high.astype(F32)).astype(BF)], axis=1)
        den = jnp.dot(both, span, preferred_element_type=F32) + den_ref[half, rows, :] + count
        num = jnp.dot(f, weights[...], preferred_element_type=F32)
        obuf[rows, :] = ((num + num_ref[half, rows, :] + vsum) / den).astype(BF)
        yield pl.ds(n * step, step)


SCALE = 1.0 / (math.sqrt(WDIM) * math.log(2.0))
QB = 2 * WINDOW


def masks():
    row, lane = rows_of((QB, QB)), lanes((QB, QB))
    earlier = (row < WINDOW) & (lane >= WINDOW)
    key = jnp.where(earlier, lane, lane + QB) - QB
    return earlier, (key <= row) & (key > row - WINDOW)


def attend(blocks, earlier, bias):
    s = jnp.stack(
        [
            lax.dot_general(q, k, (((1,), (1,)), ((), ())), preferred_element_type=F32)
            for q, k, v in blocks
        ]
    )
    s = jnp.where(earlier, s[:, :, :QB], s[:, :, QB:]) * SCALE + bias
    e = jnp.exp2(s - jnp.max(s, axis=2, keepdims=True))
    inverse = 1.0 / jnp.sum(e, axis=2, keepdims=True)
    e = jnp.concatenate([jnp.where(earlier, e, 0.0), jnp.where(earlier, 0.0, e)], axis=2).astype(BF)
    return [
        (jnp.dot(e[n], v, preferred_element_type=F32) * inverse[n]).astype(BF)
        for n, (q, k, v) in enumerate(blocks)
    ]


def window_kernel(q_ref, k_ref, v_ref, o_ref, done):
    done[...] = jnp.zeros_like(done)
    earlier, allowed = masks()
    bias = jnp.where(allowed, 0.0, -jnp.inf)
    tok, wide = q_ref.shape
    for h in range(0, wide, GROUP * WDIM):
        places = [
            (slice(at, at + QB), slice(at - QB, at + QB), slice(c, c + WDIM))
            for c in range(h, h + GROUP * WDIM, WDIM)
            for at in range(QB, tok, QB)
        ]
        outs = attend(
            [(q_ref[rows, c], k_ref[keys, c], v_ref[keys, c]) for rows, keys, c in places],
            earlier,
            bias,
        )
        for (rows, _, c), out in zip(places, outs):
            o_ref[rows, c] = out


def narrow_weights(q_ref, first_row, k_of, bias, put):
    group = 2 * GROUP * WDIM
    rows = slice(first_row, first_row + WINDOW)
    for h in range(0, q_ref.shape[1], group):
        places = [slice(c, c + WDIM) for c in range(h, h + group, WDIM)]
        s = jnp.stack(
            [
                lax.dot_general(
                    q_ref[rows, c], k_of(c), (((1,), (1,)), ((), ())), preferred_element_type=F32
                )
                for c in places
            ]
        )
        s = s * SCALE + bias
        e = jnp.exp2(s - jnp.max(s, axis=2, keepdims=True))
        e = (e * (1.0 / jnp.sum(e, axis=2, keepdims=True))).astype(BF)
        for n, c in enumerate(places):
            put(c, e[n])


def band():
    key, query = lanes((WINDOW, QB)), rows_of((WINDOW, QB))
    return (key > query) & (key <= query + WINDOW)


def query_kernel(x_ref, order_ref, f_ref, done):
    done[...] = jnp.zeros_like(done)
    for p, pair in enumerate(feature_pairs(x_ref[...], order_ref[...], COEF)):
        for half, f in enumerate(pair):
            f_ref[half, :, p * 128 : (p + 1) * 128] = f.astype(BF)


def top_kernel(q_ref, k_ref, v_ref, kh_ref, rest_ref, w_ref, o_hbm, done, obuf, sems):
    done[...] = jnp.zeros_like(done)
    allowed = band()
    rows = pl.ds(QB, q_ref.shape[0] - QB)
    copies = [pltpu.make_async_copy(rest_ref.at[rows], o_hbm.at[rows], sems.at[0])]
    copies[0].start()

    def put(c, w):
        obuf[:, c] = jnp.dot(w, v_ref[:QB, c], preferred_element_type=F32).astype(BF)

    narrow_weights(
        q_ref, WINDOW, lambda c: k_ref[:QB, c], jnp.where(allowed, 0.0, -jnp.inf), put
    )
    copies.append(pltpu.make_async_copy(obuf, o_hbm.at[pl.ds(WINDOW, WINDOW)], sems.at[1]))
    copies[1].start()
    follows = lax.axis_index("seq") > 0
    bias = jnp.where(allowed & ((lanes(allowed.shape) >= WINDOW) | follows), 0.0, -jnp.inf)

    def keep(c, w):
        w_ref[:, c] = w

    narrow_weights(
        q_ref, 0, lambda c: jnp.concatenate([kh_ref[:, c], k_ref[:WINDOW, c]], axis=0), bias, keep
    )
    for copy in copies:
        copy.wait()


def own_kernel(
    f_ref, e_ref, peer_ref, num_ref, den_ref, w_ref, v_ref, vh_ref, o_ref, top_ref, weights
):
    half = lax.axis_index("seq") % 2
    for rows in finish_half(half, f_ref, e_ref, peer_ref, num_ref, den_ref, o_ref, weights):
        pass
    for c in range(0, w_ref.shape[1], WDIM):
        c = slice(c, c + WDIM)
        v = jnp.concatenate([vh_ref[:, c], v_ref[:WINDOW, c]], axis=0)
        top_ref[:, c] = jnp.dot(w_ref[:, c], v, preferred_element_type=F32).astype(BF)


def tail_kernel(
    f_ref, e_ref, peer_ref, num_ref, den_ref, own_ref, top_ref, whole_ref,
    lin_hbm, win_hbm, weights, obuf, sems,
):
    half = lax.axis_index("seq") % 2

    def put(ref, side, at, sem):
        copy = pltpu.make_async_copy(
            ref, lin_hbm.at[at, pl.ds(pl.multiple_of(side * 256, 256), 256)], sem
        )
        copy.start()
        return copy

    copies = [
        pltpu.make_async_copy(top_ref, win_hbm.at[pl.ds(0, WINDOW)], sems.at[5]),
        put(own_ref, half, pl.ds(0, f_ref.shape[1]), sems.at[4]),
    ]
    copies[0].start()
    for n, rows in enumerate(
        finish_half(1 - half, f_ref, e_ref, peer_ref, num_ref, den_ref, obuf, weights)
    ):
        copies.append(put(obuf.at[rows], 1 - half, rows, sems.at[n]))
    for copy in copies:
        copy.wait()


def call(kernel, out, *args, in_specs, after=(), flops=0, nbytes=0, vmem=8, **kw):
    given = len(args)

    def run(*refs):
        kernel(*refs[:given], *refs[given + len(after) :])

    return pl.pallas_call(
        run,
        out_shape=out,
        in_specs=list(in_specs) + [pl.BlockSpec(memory_space=pl.ANY)] * len(after),
        cost_estimate=pl.CostEstimate(flops=flops, bytes_accessed=nbytes, transcendentals=0),
        compiler_params=pltpu.CompilerParams(vmem_limit_bytes=vmem << 20),
        name=kernel.__name__,
        **kw,
    )(*args, *after)


def exchange(x, step):
    count = lax.axis_size("seq")
    return lax.ppermute(x, "seq", [(i, i ^ step) for i in range(count)])


def shape(*dims, dtype=BF):
    return jax.ShapeDtypeStruct(dims, dtype)


def body(q_lin, k_lin, v_lin, q_win, k_win, v_win):
    tok = q_lin.shape[0]
    count = lax.axis_size("seq")
    assert count & (count - 1) == 0 and count > 1
    me = lax.axis_index("seq")
    bits = [(me & (1 << n)) != 0 for n in range(count.bit_length() - 1)]
    bits, k_lin = lax.optimization_barrier((bits, k_lin))
    wide = WHEADS * WDIM
    hbm = pl.BlockSpec(memory_space=pltpu.HBM)

    state, key_edge, val_edge, q_lin, k_lin, v_lin, order = call(
        state_kernel,
        (
            shape(2, ROWS, 128),
            shape(WINDOW, wide),
            shape(WINDOW, wide),
            shape(*q_lin.shape),
            shape(*k_lin.shape),
            shape(*v_lin.shape),
            shape(128, (1 + PAIRS) * 256),
        ),
        *(pltpu.with_memory_space_constraint(x, pltpu.HBM) for x in (q_lin, k_lin, v_lin, k_win, v_win)),
        in_specs=[hbm] * 5,
        out_specs=(VMEM,) * 7,
        scratch_shapes=[pltpu.VMEM((2, tok, PAIRS * 128), BF), pltpu.SemaphoreType.DMA((5,))],
        flops=1 << 30,
        nbytes=2 << 20,
    )

    def ring(x, after):
        x, after = lax.optimization_barrier((x, after))
        return lax.ppermute(x, "seq", [(i, (i + 1) % count) for i in range(count)]), after

    peer = exchange(state, 1)
    token = shape(8, 128, dtype=F32)
    feats, first = call(
        query_kernel,
        (shape(2, tok, PAIRS * 128), token),
        q_lin,
        order,
        after=(state,),
        in_specs=[VMEM] * 2,
        out_specs=(VMEM, VMEM),
        flops=1 << 28,
        nbytes=2 << 20,
    )
    done = (first,)
    peer, done = lax.optimization_barrier((peer, done))
    both = state.astype(F32) + peer.astype(F32)
    carried = jnp.where(bits[0], both[1], both[0])
    before = jnp.zeros_like(carried)

    def local(after):
        num, den, done = call(
            local_kernel,
            (shape(2, tok, HEADS * VDIM // 2, dtype=F32),) * 2 + (token,),
            q_lin,
            k_lin,
            v_lin,
            after=after,
            in_specs=[VMEM] * 3,
            out_specs=(VMEM,) * 3,
            flops=1 << 31,
            nbytes=3 << 20,
        )
        return (num, den), (done,)

    def window(after):
        win, done = call(
            window_kernel,
            (shape(tok, wide), token),
            q_win,
            k_win,
            v_win,
            after=after,
            in_specs=[VMEM] * 3,
            out_specs=(VMEM, VMEM),
            flops=1 << 31,
            nbytes=8 << 20,
        )
        return win, (done,)

    def top(after, win):
        shares, win, done = call(
            top_kernel,
            (shape(WINDOW, wide), shape(tok, wide), token),
            q_win,
            k_win,
            v_win,
            key_edge,
            win,
            after=after,
            in_specs=[VMEM] * 5,
            out_specs=(VMEM, hbm, VMEM),
            scratch_shapes=[
                pltpu.VMEM((WINDOW, wide), BF),
                pltpu.SemaphoreType.DMA((2,)),
            ],
            flops=1 << 30,
            nbytes=2 << 20,
        )
        return shares, win, (done,)

    step, turn = 2, 0
    sums = win = shares = None
    while step < count:
        send = carried.astype(BF)
        if turn == 0:
            key_edge, send = ring(key_edge, send)
        elif turn == 1:
            val_edge, send = ring(val_edge, send)
        got = exchange(send, step + step // 2 if 2 * step == count else step)
        after = (send,) + done
        if turn == 0:
            sums, done = local(after)
        elif turn == 1:
            win, done = window(after)
        elif turn == 2:
            shares, win, done = top(after, win)
        if turn == 2:
            got, done, val_edge = lax.optimization_barrier((got, done, val_edge))
        elif turn < 2:
            got, done = lax.optimization_barrier((got, done))
        got = got.astype(F32)
        before = before + jnp.where(bits[turn + 1], got, 0.0)
        carried = carried + got
        step *= 2
        turn += 1
    assert turn >= 3
    own = before.astype(BF)
    other = exchange(own, 1)
    weights = pltpu.VMEM((PAIRS * 128, 256), BF)
    mine, top = call(
        own_kernel,
        (shape(tok, HEADS * VDIM // 2), shape(WINDOW, wide)),
        feats,
        own,
        peer,
        *sums,
        shares,
        v_win,
        val_edge,
        after=done,
        in_specs=[VMEM] * 8,
        out_specs=(VMEM, VMEM),
        scratch_shapes=[weights],
        flops=1 << 30,
        nbytes=3 << 20,
    )
    other, mine, top = lax.optimization_barrier((other, mine, top))
    return call(
        tail_kernel,
        (shape(tok, HEADS * VDIM), shape(tok, wide)),
        feats,
        other,
        peer,
        *sums,
        mine,
        top,
        win,
        in_specs=[VMEM] * 7 + [hbm],
        out_specs=(hbm, hbm),
        scratch_shapes=[
            weights,
            pltpu.VMEM((tok, HEADS * VDIM // 2), BF),
            pltpu.SemaphoreType.DMA((6,)),
        ],
        input_output_aliases={7: 1},
        flops=1 << 29,
        nbytes=2 << 20,
    )


def solution(mesh):
    spec = P(("groups", "seq"), None)
    return jax.shard_map(
        body, mesh=mesh, in_specs=(spec,) * 6, out_specs=(spec, spec), check_vma=False
    )
```

```python
import math

import jax
import jax.numpy as jnp
from jax import lax
from jax.experimental import pallas as pl
from jax.experimental.pallas import tpu as pltpu
from jax.sharding import PartitionSpec as P

HEADS = 8
KDIM = 16
VDIM = 64
WHEADS = 16
WDIM = 128
WINDOW = 64

BF = jnp.bfloat16
F32 = jnp.float32
BLOCKS = 10
PAIRS = BLOCKS // 2
MAIN = PAIRS * 64
ROWS = MAIN + 16
STEP = 256
GROUP = 4
COEF = (1 / 32,) + (1 / 16,) * 7 + (1 / 32, 1 / 4)
VMEM = pl.BlockSpec(memory_space=pltpu.VMEM)


def lanes(shape):
    return lax.broadcasted_iota(jnp.int32, shape, len(shape) - 1)


def rows_of(shape):
    return lax.broadcasted_iota(jnp.int32, shape, len(shape) - 2)


def orders():
    dims = (128, (1 + PAIRS) * 256)
    src, dst = rows_of(dims), lanes(dims)
    d = jnp.where(dst < 256, 0, dst // 256 * 2 - 2 + dst % 128 // 64)
    head, entry = dst % 256 // 128 * 4 + dst % 4, (dst % 64 // 4 + d) % KDIM
    return (src == head * KDIM + entry).astype(BF)


def feature_pairs(x, order, coef):
    own = jnp.dot(x, order[:, :256], preferred_element_type=F32)
    others = jnp.dot(x, order[:, 256:], preferred_element_type=F32)
    left = lanes((x.shape[0], 128)) < 64
    for p in range(PAIRS):
        pair = []
        for half in range(2):
            at = p * 256 + half * 128
            other = others[:, at : at + 128]
            if p == PAIRS - 1:
                other = jnp.where(left, other, 1.0)
            f = own[:, half * 128 : (half + 1) * 128] * other
            if coef is not None:
                low, high = coef[2 * p : 2 * p + 2]
                f = f * (low if low == high else jnp.where(left[:1], low, high))
            pair.append(f)
        yield pair


def state_kernel(
    q_hbm, k_hbm, v_hbm, kw_hbm, vw_hbm,
    s_ref, ke_ref, ve_ref, q_ref, k_ref, v_ref, order_ref, f_ref, sems,
):
    last = pl.ds(kw_hbm.shape[0] - WINDOW, WINDOW)
    moves = (
        (k_hbm, k_ref),
        (v_hbm, v_ref),
        (kw_hbm.at[last], ke_ref),
        (q_hbm, q_ref),
        (vw_hbm.at[last], ve_ref),
    )
    copies = [pltpu.make_async_copy(src, dst, sems.at[n]) for n, (src, dst) in enumerate(moves)]
    for copy in copies:
        copy.start()
    order_ref[...] = orders()
    core = lax.axis_index("seq") % 2
    copies[0].wait()
    sums = []
    for p, pair in enumerate(feature_pairs(k_ref[...], order_ref[...], None)):
        sums.append([jnp.sum(f, axis=0, keepdims=True) for f in pair])
        for half, f in enumerate(pair):
            f_ref[half, :, p * 128 : (p + 1) * 128] = f.astype(BF)
    copies[1].wait()
    v = v_ref[...]
    vsum = jnp.sum(v.astype(F32), axis=0, keepdims=True)
    left = lanes((64, 128)) < 64
    head = rows_of((64, 128)) % 4
    for half in range(2):
        slot = (core + half) % 2
        r = lax.dot_general(
            f_ref[half],
            v[:, half * 256 : (half + 1) * 256],
            (((0,), (0,)), ((), ())),
            preferred_element_type=F32,
        )
        for p in range(PAIRS):
            pieces = []
            for par in range(2):
                at = p * 128 + par * 64
                z = jnp.where(head < 2, r[at : at + 64, :128], r[at : at + 64, 128:])
                pieces.append(jnp.where(head % 2 == par, z, pltpu.roll(z, 64, 1)))
            s_ref[slot, p * 64 : (p + 1) * 64, :] = jnp.where(left, *pieces).astype(BF)
        aux = [total[half] for total in sums]
        aux += [vsum[:, half * 256 + t * 128 : half * 256 + (t + 1) * 128] for t in range(2)]
        aux.append(jnp.zeros((ROWS - MAIN - PAIRS - 2, 128), F32))
        s_ref[slot, MAIN:, :] = jnp.concatenate(aux, axis=0).astype(BF)
    for copy in copies[2:]:
        copy.wait()


def local_kernel(q_ref, k_ref, v_ref, num_ref, den_ref, done):
    done[...] = jnp.zeros_like(done)
    tok = q_ref.shape[0]
    step = STEP
    k = k_ref[...]
    lane = lanes((step, 128))
    left = lane < 64
    left_all = lanes((tok, 128)) < 64
    causal = rows_of((step, step)) >= lanes((step, step))
    one = jnp.ones((tok, 128), BF)
    for r in range(tok // step):
        rows, end = slice(r * step, (r + 1) * step), (r + 1) * step
        q = q_ref[rows, :]
        for t0 in range(0, HEADS // 2, 2):
            places = [(t, e) for t in (t0, t0 + 1) for e in range(2)]
            kernels = []
            for t, e in places:
                qm = jnp.where(lane // KDIM == 2 * t + e, q, jnp.zeros_like(q))
                u = lax.dot_general(
                    qm, k[:end, :], (((1,), (1,)), ((), ())), preferred_element_type=F32
                )
                kernels.append(u + 4.0)
            outs = []
            for w, (t, e) in zip(kernels, places):
                w = w * w * (1 / 32) + 0.5
                diag = jnp.where(causal, w[:, r * step :], 0.0).astype(BF)
                if r:
                    diag = jnp.concatenate([w[:, : r * step].astype(BF), diag], axis=1)
                v = v_ref[:, t * 128 : (t + 1) * 128]
                aug = jnp.where(left_all, one, v) if e else jnp.where(left_all, v, one)
                outs.append(jnp.dot(diag, aug[:end, :], preferred_element_type=F32))
            for n in range(2):
                half, cols = t0 // 2, slice(n * 128, (n + 1) * 128)
                a, b = outs[2 * n : 2 * n + 2]
                num_ref[half, rows, cols] = jnp.where(left, a, b)
                den_ref[half, rows, cols] = pltpu.roll(jnp.where(left, b, a), 64, 1)


def finish_half(half, f_ref, e_ref, num_ref, den_ref, obuf, weights):
    tok = f_ref.shape[1]
    me = lax.axis_index("seq")
    left = lanes((64, 128)) < 64
    row = rows_of((64, 128)) % 4
    col = lanes((64, 128)) // VDIM
    span = (rows_of((256, 256)) % 4 == lanes((256, 256)) // VDIM).astype(BF)
    count = (me * tok).astype(F32)
    state = e_ref[...].astype(F32)
    for p in range(PAIRS):
        c = state[p * 64 : (p + 1) * 64, :]
        turned = pltpu.roll(c, 64, 1)
        for par in range(2):
            base = jnp.where(left, c, turned) if par == 0 else jnp.where(left, turned, c)
            at = p * 128 + par * 64
            for t in range(2):
                weights[at : at + 64, t * 128 : (t + 1) * 128] = jnp.where(
                    row == col + 2 * t, base, 0.0
                ).astype(BF)
    at = MAIN + PAIRS
    vsum = jnp.concatenate([state[at : at + 1, :], state[at + 1 : at + 2, :]], axis=1)
    step = tok // 4
    for n in range(tok // step):
        rows = slice(n * step, (n + 1) * step)
        f = f_ref[half, rows, :]
        acc = jnp.zeros((step, 128), F32)
        for p in range(PAIRS):
            z = state[MAIN + p : MAIN + p + 1, :]
            acc = acc + f[:, p * 128 : (p + 1) * 128].astype(F32) * z
        high = acc.astype(BF)
        both = jnp.concatenate([high, (acc - high.astype(F32)).astype(BF)], axis=1)
        den = jnp.dot(both, span, preferred_element_type=F32) + den_ref[half, rows, :] + count
        num = jnp.dot(f, weights[...], preferred_element_type=F32)
        obuf[rows, :] = ((num + num_ref[half, rows, :] + vsum) / den).astype(BF)
        yield pl.ds(n * step, step)


SCALE = 1.0 / (math.sqrt(WDIM) * math.log(2.0))
QB = 2 * WINDOW


def masks():
    row, lane = rows_of((QB, QB)), lanes((QB, QB))
    earlier = (row < WINDOW) & (lane >= WINDOW)
    key = jnp.where(earlier, lane, lane + QB) - QB
    return earlier, (key <= row) & (key > row - WINDOW)


def attend(blocks, earlier, bias):
    s = jnp.stack(
        [
            lax.dot_general(q, k, (((1,), (1,)), ((), ())), preferred_element_type=F32)
            for q, k, v in blocks
        ]
    )
    s = jnp.where(earlier, s[:, :, :QB], s[:, :, QB:]) * SCALE + bias
    e = jnp.exp2(s - jnp.max(s, axis=2, keepdims=True))
    inverse = 1.0 / jnp.sum(e, axis=2, keepdims=True)
    e = jnp.concatenate([jnp.where(earlier, e, 0.0), jnp.where(earlier, 0.0, e)], axis=2).astype(BF)
    return [
        (jnp.dot(e[n], v, preferred_element_type=F32) * inverse[n]).astype(BF)
        for n, (q, k, v) in enumerate(blocks)
    ]


def window_kernel(q_ref, k_ref, v_ref, o_ref, done):
    done[...] = jnp.zeros_like(done)
    earlier, allowed = masks()
    bias = jnp.where(allowed, 0.0, -jnp.inf)
    tok, wide = q_ref.shape
    for h in range(0, wide, GROUP * WDIM):
        places = [
            (slice(at, at + QB), slice(at - QB, at + QB), slice(c, c + WDIM))
            for c in range(h, h + GROUP * WDIM, WDIM)
            for at in range(QB, tok, QB)
        ]
        outs = attend(
            [(q_ref[rows, c], k_ref[keys, c], v_ref[keys, c]) for rows, keys, c in places],
            earlier,
            bias,
        )
        for (rows, _, c), out in zip(places, outs):
            o_ref[rows, c] = out


def narrow_weights(q_ref, first_row, k_of, bias, put):
    group = 2 * GROUP * WDIM
    rows = slice(first_row, first_row + WINDOW)
    for h in range(0, q_ref.shape[1], group):
        places = [slice(c, c + WDIM) for c in range(h, h + group, WDIM)]
        s = jnp.stack(
            [
                lax.dot_general(
                    q_ref[rows, c], k_of(c), (((1,), (1,)), ((), ())), preferred_element_type=F32
                )
                for c in places
            ]
        )
        s = s * SCALE + bias
        e = jnp.exp2(s - jnp.max(s, axis=2, keepdims=True))
        e = (e * (1.0 / jnp.sum(e, axis=2, keepdims=True))).astype(BF)
        for n, c in enumerate(places):
            put(c, e[n])


def band():
    key, query = lanes((WINDOW, QB)), rows_of((WINDOW, QB))
    return (key > query) & (key <= query + WINDOW)


def query_kernel(x_ref, order_ref, f_ref, done):
    done[...] = jnp.zeros_like(done)
    for p, pair in enumerate(feature_pairs(x_ref[...], order_ref[...], COEF)):
        for half, f in enumerate(pair):
            f_ref[half, :, p * 128 : (p + 1) * 128] = f.astype(BF)


def top_kernel(q_ref, k_ref, v_ref, kh_ref, rest_ref, w_ref, o_hbm, done, obuf, sems):
    done[...] = jnp.zeros_like(done)
    allowed = band()
    rows = pl.ds(QB, q_ref.shape[0] - QB)
    copies = [pltpu.make_async_copy(rest_ref.at[rows], o_hbm.at[rows], sems.at[0])]
    copies[0].start()

    def put(c, w):
        obuf[:, c] = jnp.dot(w, v_ref[:QB, c], preferred_element_type=F32).astype(BF)

    narrow_weights(
        q_ref, WINDOW, lambda c: k_ref[:QB, c], jnp.where(allowed, 0.0, -jnp.inf), put
    )
    copies.append(pltpu.make_async_copy(obuf, o_hbm.at[pl.ds(WINDOW, WINDOW)], sems.at[1]))
    copies[1].start()
    follows = lax.axis_index("seq") > 0
    bias = jnp.where(allowed & ((lanes(allowed.shape) >= WINDOW) | follows), 0.0, -jnp.inf)

    def keep(c, w):
        w_ref[:, c] = w

    narrow_weights(
        q_ref, 0, lambda c: jnp.concatenate([kh_ref[:, c], k_ref[:WINDOW, c]], axis=0), bias, keep
    )
    for copy in copies:
        copy.wait()


def own_kernel(
    f_ref, e_ref, num_ref, den_ref, w_ref, v_ref, vh_ref, o_ref, top_ref, weights
):
    half = lax.axis_index("seq") % 2
    for rows in finish_half(half, f_ref, e_ref, num_ref, den_ref, o_ref, weights):
        pass
    for c in range(0, w_ref.shape[1], WDIM):
        c = slice(c, c + WDIM)
        v = jnp.concatenate([vh_ref[:, c], v_ref[:WINDOW, c]], axis=0)
        top_ref[:, c] = jnp.dot(w_ref[:, c], v, preferred_element_type=F32).astype(BF)


def tail_kernel(
    f_ref, e_ref, num_ref, den_ref, own_ref, top_ref, whole_ref,
    lin_hbm, win_hbm, weights, obuf, sems,
):
    half = lax.axis_index("seq") % 2

    def put(ref, side, at, sem):
        copy = pltpu.make_async_copy(
            ref, lin_hbm.at[at, pl.ds(pl.multiple_of(side * 256, 256), 256)], sem
        )
        copy.start()
        return copy

    copies = [
        pltpu.make_async_copy(top_ref, win_hbm.at[pl.ds(0, WINDOW)], sems.at[5]),
        put(own_ref, half, pl.ds(0, f_ref.shape[1]), sems.at[4]),
    ]
    copies[0].start()
    for n, rows in enumerate(
        finish_half(1 - half, f_ref, e_ref, num_ref, den_ref, obuf, weights)
    ):
        copies.append(put(obuf.at[rows], 1 - half, rows, sems.at[n]))
    for copy in copies:
        copy.wait()


def call(kernel, out, *args, in_specs, after=(), flops=0, nbytes=0, vmem=8, **kw):
    given = len(args)

    def run(*refs):
        kernel(*refs[:given], *refs[given + len(after) :])

    return pl.pallas_call(
        run,
        out_shape=out,
        in_specs=list(in_specs) + [pl.BlockSpec(memory_space=pl.ANY)] * len(after),
        cost_estimate=pl.CostEstimate(flops=flops, bytes_accessed=nbytes, transcendentals=0),
        compiler_params=pltpu.CompilerParams(vmem_limit_bytes=vmem << 20),
        name=kernel.__name__,
        **kw,
    )(*args, *after)


def exchange(x, step):
    count = lax.axis_size("seq")
    return lax.ppermute(x, "seq", [(i, i ^ step) for i in range(count)])


def shape(*dims, dtype=BF):
    return jax.ShapeDtypeStruct(dims, dtype)


def body(q_lin, k_lin, v_lin, q_win, k_win, v_win):
    tok = q_lin.shape[0]
    count = lax.axis_size("seq")
    assert count & (count - 1) == 0 and count > 1
    me = lax.axis_index("seq")
    bits = [(me & (1 << n)) != 0 for n in range(count.bit_length() - 1)]
    bits, k_lin = lax.optimization_barrier((bits, k_lin))
    wide = WHEADS * WDIM
    hbm = pl.BlockSpec(memory_space=pltpu.HBM)

    state, key_edge, val_edge, q_lin, k_lin, v_lin, order = call(
        state_kernel,
        (
            shape(2, ROWS, 128),
            shape(WINDOW, wide),
            shape(WINDOW, wide),
            shape(*q_lin.shape),
            shape(*k_lin.shape),
            shape(*v_lin.shape),
            shape(128, (1 + PAIRS) * 256),
        ),
        *(pltpu.with_memory_space_constraint(x, pltpu.HBM) for x in (q_lin, k_lin, v_lin, k_win, v_win)),
        in_specs=[hbm] * 5,
        out_specs=(VMEM,) * 7,
        scratch_shapes=[pltpu.VMEM((2, tok, PAIRS * 128), BF), pltpu.SemaphoreType.DMA((5,))],
        flops=1 << 30,
        nbytes=2 << 20,
    )

    def ring(x, after):
        x, after = lax.optimization_barrier((x, after))
        return lax.ppermute(x, "seq", [(i, (i + 1) % count) for i in range(count)]), after

    peer = exchange(state[1], 1)
    token = shape(8, 128, dtype=F32)
    feats, first = call(
        query_kernel,
        (shape(2, tok, PAIRS * 128), token),
        q_lin,
        order,
        after=(state,),
        in_specs=[VMEM] * 2,
        out_specs=(VMEM, VMEM),
        flops=1 << 28,
        nbytes=2 << 20,
    )
    done = (first,)
    peer, done = lax.optimization_barrier((peer, done))
    mine, peer = state[0].astype(F32), peer.astype(F32)
    carried = mine + peer
    before = jnp.zeros_like(carried)

    def local(after):
        num, den, done = call(
            local_kernel,
            (shape(2, tok, HEADS * VDIM // 2, dtype=F32),) * 2 + (token,),
            q_lin,
            k_lin,
            v_lin,
            after=after,
            in_specs=[VMEM] * 3,
            out_specs=(VMEM,) * 3,
            flops=1 << 31,
            nbytes=3 << 20,
        )
        return (num, den), (done,)

    def window(after):
        win, done = call(
            window_kernel,
            (shape(tok, wide), token),
            q_win,
            k_win,
            v_win,
            after=after,
            in_specs=[VMEM] * 3,
            out_specs=(VMEM, VMEM),
            flops=1 << 31,
            nbytes=8 << 20,
        )
        return win, (done,)

    def top(after, win):
        shares, win, done = call(
            top_kernel,
            (shape(WINDOW, wide), shape(tok, wide), token),
            q_win,
            k_win,
            v_win,
            key_edge,
            win,
            after=after,
            in_specs=[VMEM] * 5,
            out_specs=(VMEM, hbm, VMEM),
            scratch_shapes=[
                pltpu.VMEM((WINDOW, wide), BF),
                pltpu.SemaphoreType.DMA((2,)),
            ],
            flops=1 << 30,
            nbytes=2 << 20,
        )
        return shares, win, (done,)

    step, turn = 2, 0
    sums = win = shares = None
    while step < count:
        send = carried.astype(BF)
        if turn == 0:
            key_edge, send = ring(key_edge, send)
        elif turn == 1:
            val_edge, send = ring(val_edge, send)
        got = exchange(send, step + step // 2 if 2 * step == count else step)
        after = (send,) + done
        if turn == 0:
            sums, done = local(after)
        elif turn == 1:
            win, done = window(after)
        elif turn == 2:
            shares, win, done = top(after, win)
        if turn == 2:
            got, done, val_edge = lax.optimization_barrier((got, done, val_edge))
        elif turn < 2:
            got, done = lax.optimization_barrier((got, done))
        got = got.astype(F32)
        before = before + jnp.where(bits[turn + 1], got, 0.0)
        carried = carried + got
        step *= 2
        turn += 1
    assert turn >= 3
    own = (before + jnp.where(bits[0], peer, 0.0)).astype(BF)
    other = exchange((before + jnp.where(bits[0], 0.0, mine)).astype(BF), 1)
    weights = pltpu.VMEM((PAIRS * 128, 256), BF)
    mine, top = call(
        own_kernel,
        (shape(tok, HEADS * VDIM // 2), shape(WINDOW, wide)),
        feats,
        own,
        *sums,
        shares,
        v_win,
        val_edge,
        after=done,
        in_specs=[VMEM] * 7,
        out_specs=(VMEM, VMEM),
        scratch_shapes=[weights],
        flops=1 << 30,
        nbytes=3 << 20,
    )
    other, mine, top = lax.optimization_barrier((other, mine, top))
    return call(
        tail_kernel,
        (shape(tok, HEADS * VDIM), shape(tok, wide)),
        feats,
        other,
        *sums,
        mine,
        top,
        win,
        in_specs=[VMEM] * 6 + [hbm],
        out_specs=(hbm, hbm),
        scratch_shapes=[
            weights,
            pltpu.VMEM((tok, HEADS * VDIM // 2), BF),
            pltpu.SemaphoreType.DMA((6,)),
        ],
        input_output_aliases={6: 1},
        flops=1 << 29,
        nbytes=2 << 20,
    )


def solution(mesh):
    spec = P(("groups", "seq"), None)
    return jax.shard_map(
        body, mesh=mesh, in_specs=(spec,) * 6, out_specs=(spec, spec), check_vma=False
    )
```

```python
import math

import jax
import jax.numpy as jnp
from jax import lax
from jax.experimental import pallas as pl
from jax.experimental.pallas import tpu as pltpu
from jax.sharding import PartitionSpec as P

HEADS = 8
KDIM = 16
VDIM = 64
WHEADS = 16
WDIM = 128
WINDOW = 64

BF = jnp.bfloat16
F32 = jnp.float32
BLOCKS = 10
PAIRS = BLOCKS // 2
MAIN = PAIRS * 64
ROWS = MAIN + 16
STEP = 256
GROUP = 4
COEF = (1 / 32,) + (1 / 16,) * 7 + (1 / 32, 1 / 4)
VMEM = pl.BlockSpec(memory_space=pltpu.VMEM)


def lanes(shape):
    return lax.broadcasted_iota(jnp.int32, shape, len(shape) - 1)


def rows_of(shape):
    return lax.broadcasted_iota(jnp.int32, shape, len(shape) - 2)


def orders():
    dims = (128, (1 + PAIRS) * 256)
    src, dst = rows_of(dims), lanes(dims)
    d = jnp.where(dst < 256, 0, dst // 256 * 2 - 2 + dst % 128 // 64)
    head, entry = dst % 256 // 128 * 4 + dst % 4, (dst % 64 // 4 + d) % KDIM
    return (src == head * KDIM + entry).astype(BF)


def feature_pairs(x, order, coef):
    own = jnp.dot(x, order[:, :256], preferred_element_type=F32)
    others = jnp.dot(x, order[:, 256:], preferred_element_type=F32)
    left = lanes((x.shape[0], 128)) < 64
    for p in range(PAIRS):
        pair = []
        for half in range(2):
            at = p * 256 + half * 128
            other = others[:, at : at + 128]
            if p == PAIRS - 1:
                other = jnp.where(left, other, 1.0)
            f = own[:, half * 128 : (half + 1) * 128] * other
            if coef is not None:
                low, high = coef[2 * p : 2 * p + 2]
                f = f * (low if low == high else jnp.where(left[:1], low, high))
            pair.append(f)
        yield pair


def state_kernel(
    q_hbm, k_hbm, v_hbm, kw_hbm, vw_hbm,
    s_ref, ke_ref, ve_ref, q_ref, k_ref, v_ref, order_ref, f_ref, sems,
):
    last = pl.ds(kw_hbm.shape[0] - WINDOW, WINDOW)
    moves = (
        (k_hbm, k_ref),
        (v_hbm, v_ref),
        (kw_hbm.at[last], ke_ref),
        (q_hbm, q_ref),
        (vw_hbm.at[last], ve_ref),
    )
    copies = [pltpu.make_async_copy(src, dst, sems.at[n]) for n, (src, dst) in enumerate(moves)]
    for copy in copies:
        copy.start()
    order_ref[...] = orders()
    copies[0].wait()
    sums = []
    for p, pair in enumerate(feature_pairs(k_ref[...], order_ref[...], None)):
        sums.append([jnp.sum(f, axis=0, keepdims=True) for f in pair])
        for half, f in enumerate(pair):
            f_ref[half, :, p * 128 : (p + 1) * 128] = f.astype(BF)
    copies[1].wait()
    v = v_ref[...]
    vsum = jnp.sum(v.astype(F32), axis=0, keepdims=True)
    left = lanes((64, 128)) < 64
    head = rows_of((64, 128)) % 4
    for half in range(2):
        r = lax.dot_general(
            f_ref[half],
            v[:, half * 256 : (half + 1) * 256],
            (((0,), (0,)), ((), ())),
            preferred_element_type=F32,
        )
        for p in range(PAIRS):
            pieces = []
            for par in range(2):
                at = p * 128 + par * 64
                z = jnp.where(head < 2, r[at : at + 64, :128], r[at : at + 64, 128:])
                pieces.append(jnp.where(head % 2 == par, z, pltpu.roll(z, 64, 1)))
            s_ref[half, p * 64 : (p + 1) * 64, :] = jnp.where(left, *pieces).astype(BF)
        aux = [total[half] for total in sums]
        aux += [vsum[:, half * 256 + t * 128 : half * 256 + (t + 1) * 128] for t in range(2)]
        aux.append(jnp.zeros((ROWS - MAIN - PAIRS - 2, 128), F32))
        s_ref[half, MAIN:, :] = jnp.concatenate(aux, axis=0).astype(BF)
    for copy in copies[2:]:
        copy.wait()


def local_kernel(q_ref, k_ref, v_ref, num_ref, den_ref, done):
    done[...] = jnp.zeros_like(done)
    tok = q_ref.shape[0]
    step = STEP
    k = k_ref[...]
    lane = lanes((step, 128))
    left = lane < 64
    left_all = lanes((tok, 128)) < 64
    causal = rows_of((step, step)) >= lanes((step, step))
    one = jnp.ones((tok, 128), BF)
    for r in range(tok // step):
        rows, end = slice(r * step, (r + 1) * step), (r + 1) * step
        q = q_ref[rows, :]
        for t0 in range(0, HEADS // 2, 2):
            places = [(t, e) for t in (t0, t0 + 1) for e in range(2)]
            kernels = []
            for t, e in places:
                qm = jnp.where(lane // KDIM == 2 * t + e, q, jnp.zeros_like(q))
                u = lax.dot_general(
                    qm, k[:end, :], (((1,), (1,)), ((), ())), preferred_element_type=F32
                )
                kernels.append(u + 4.0)
            outs = []
            for w, (t, e) in zip(kernels, places):
                w = w * w + 16.0
                diag = jnp.where(causal, w[:, r * step :], 0.0).astype(BF)
                if r:
                    diag = jnp.concatenate([w[:, : r * step].astype(BF), diag], axis=1)
                v = v_ref[:, t * 128 : (t + 1) * 128]
                aug = jnp.where(left_all, one, v) if e else jnp.where(left_all, v, one)
                outs.append(jnp.dot(diag, aug[:end, :], preferred_element_type=F32))
            for n in range(2):
                half, cols = t0 // 2, slice(n * 128, (n + 1) * 128)
                a, b = (out * (1 / 32) for out in outs[2 * n : 2 * n + 2])
                num_ref[half, rows, cols] = jnp.where(left, a, b)
                den_ref[half, rows, cols] = pltpu.roll(jnp.where(left, b, a), 64, 1)


def finish_half(half, f_ref, e_ref, peer_ref, num_ref, den_ref, obuf, weights):
    tok = f_ref.shape[1]
    me = lax.axis_index("seq")
    core = me % 2
    left = lanes((64, 128)) < 64
    row = rows_of((64, 128)) % 4
    col = lanes((64, 128)) // VDIM
    span = (rows_of((256, 256)) % 4 == lanes((256, 256)) // VDIM).astype(BF)
    count = (me * tok).astype(F32)
    state = e_ref[...].astype(F32) + jnp.where(core == 1, peer_ref[half].astype(F32), 0.0)
    for p in range(PAIRS):
        c = state[p * 64 : (p + 1) * 64, :]
        turned = pltpu.roll(c, 64, 1)
        for par in range(2):
            base = jnp.where(left, c, turned) if par == 0 else jnp.where(left, turned, c)
            at = p * 128 + par * 64
            for t in range(2):
                weights[at : at + 64, t * 128 : (t + 1) * 128] = jnp.where(
                    row == col + 2 * t, base, 0.0
                ).astype(BF)
    at = MAIN + PAIRS
    vsum = jnp.concatenate([state[at : at + 1, :], state[at + 1 : at + 2, :]], axis=1)
    step = tok // 4
    for n in range(tok // step):
        rows = slice(n * step, (n + 1) * step)
        f = f_ref[half, rows, :]
        acc = jnp.zeros((step, 128), F32)
        for p in range(PAIRS):
            z = state[MAIN + p : MAIN + p + 1, :]
            acc = acc + f[:, p * 128 : (p + 1) * 128].astype(F32) * z
        high = acc.astype(BF)
        both = jnp.concatenate([high, (acc - high.astype(F32)).astype(BF)], axis=1)
        den = jnp.dot(both, span, preferred_element_type=F32) + den_ref[half, rows, :] + count
        num = jnp.dot(f, weights[...], preferred_element_type=F32)
        obuf[rows, :] = ((num + num_ref[half, rows, :] + vsum) / den).astype(BF)
        yield pl.ds(n * step, step)


SCALE = 1.0 / (math.sqrt(WDIM) * math.log(2.0))
QB = 2 * WINDOW


def masks():
    row, lane = rows_of((QB, QB)), lanes((QB, QB))
    earlier = (row < WINDOW) & (lane >= WINDOW)
    key = jnp.where(earlier, lane, lane + QB) - QB
    return earlier, (key <= row) & (key > row - WINDOW)


def attend(blocks, earlier, bias):
    s = jnp.stack(
        [
            lax.dot_general(q, k, (((1,), (1,)), ((), ())), preferred_element_type=F32)
            for q, k, v in blocks
        ]
    )
    s = jnp.where(earlier, s[:, :, :QB], s[:, :, QB:]) * SCALE + bias
    e = jnp.exp2(s - jnp.max(s, axis=2, keepdims=True))
    inverse = 1.0 / jnp.sum(e, axis=2, keepdims=True)
    e = jnp.concatenate([jnp.where(earlier, e, 0.0), jnp.where(earlier, 0.0, e)], axis=2).astype(BF)
    return [
        (jnp.dot(e[n], v, preferred_element_type=F32) * inverse[n]).astype(BF)
        for n, (q, k, v) in enumerate(blocks)
    ]


def window_kernel(q_ref, k_ref, v_ref, o_ref, done):
    done[...] = jnp.zeros_like(done)
    earlier, allowed = masks()
    bias = jnp.where(allowed, 0.0, -jnp.inf)
    tok, wide = q_ref.shape
    for h in range(0, wide, GROUP * WDIM):
        places = [
            (slice(at, at + QB), slice(at - QB, at + QB), slice(c, c + WDIM))
            for c in range(h, h + GROUP * WDIM, WDIM)
            for at in range(QB, tok, QB)
        ]
        outs = attend(
            [(q_ref[rows, c], k_ref[keys, c], v_ref[keys, c]) for rows, keys, c in places],
            earlier,
            bias,
        )
        for (rows, _, c), out in zip(places, outs):
            o_ref[rows, c] = out


def narrow_weights(q_ref, first_row, k_of, bias, put):
    group = 2 * GROUP * WDIM
    rows = slice(first_row, first_row + WINDOW)
    for h in range(0, q_ref.shape[1], group):
        places = [slice(c, c + WDIM) for c in range(h, h + group, WDIM)]
        s = jnp.stack(
            [
                lax.dot_general(
                    q_ref[rows, c], k_of(c), (((1,), (1,)), ((), ())), preferred_element_type=F32
                )
                for c in places
            ]
        )
        s = s * SCALE + bias
        e = jnp.exp2(s - jnp.max(s, axis=2, keepdims=True))
        e = (e * (1.0 / jnp.sum(e, axis=2, keepdims=True))).astype(BF)
        for n, c in enumerate(places):
            put(c, e[n])


def band():
    key, query = lanes((WINDOW, QB)), rows_of((WINDOW, QB))
    return (key > query) & (key <= query + WINDOW)


def query_kernel(x_ref, order_ref, f_ref, done):
    done[...] = jnp.zeros_like(done)
    for p, pair in enumerate(feature_pairs(x_ref[...], order_ref[...], COEF)):
        for half, f in enumerate(pair):
            f_ref[half, :, p * 128 : (p + 1) * 128] = f.astype(BF)


def top_kernel(q_ref, k_ref, v_ref, kh_ref, rest_ref, w_ref, o_hbm, done, obuf, sems):
    done[...] = jnp.zeros_like(done)
    allowed = band()
    rows = pl.ds(QB, q_ref.shape[0] - QB)
    copies = [pltpu.make_async_copy(rest_ref.at[rows], o_hbm.at[rows], sems.at[0])]
    copies[0].start()

    def put(c, w):
        obuf[:, c] = jnp.dot(w, v_ref[:QB, c], preferred_element_type=F32).astype(BF)

    narrow_weights(
        q_ref, WINDOW, lambda c: k_ref[:QB, c], jnp.where(allowed, 0.0, -jnp.inf), put
    )
    copies.append(pltpu.make_async_copy(obuf, o_hbm.at[pl.ds(WINDOW, WINDOW)], sems.at[1]))
    copies[1].start()
    follows = lax.axis_index("seq") > 0
    bias = jnp.where(allowed & ((lanes(allowed.shape) >= WINDOW) | follows), 0.0, -jnp.inf)

    def keep(c, w):
        w_ref[:, c] = w

    narrow_weights(
        q_ref, 0, lambda c: jnp.concatenate([kh_ref[:, c], k_ref[:WINDOW, c]], axis=0), bias, keep
    )
    for copy in copies:
        copy.wait()


def own_kernel(
    f_ref, e_ref, peer_ref, num_ref, den_ref, w_ref, v_ref, vh_ref, o_ref, top_ref, weights
):
    half = lax.axis_index("seq") % 2
    for rows in finish_half(half, f_ref, e_ref, peer_ref, num_ref, den_ref, o_ref, weights):
        pass
    for c in range(0, w_ref.shape[1], WDIM):
        c = slice(c, c + WDIM)
        v = jnp.concatenate([vh_ref[:, c], v_ref[:WINDOW, c]], axis=0)
        top_ref[:, c] = jnp.dot(w_ref[:, c], v, preferred_element_type=F32).astype(BF)


def tail_kernel(
    f_ref, e_ref, peer_ref, num_ref, den_ref, own_ref, top_ref, whole_ref,
    lin_hbm, win_hbm, weights, obuf, sems,
):
    half = lax.axis_index("seq") % 2

    def put(ref, side, at, sem):
        copy = pltpu.make_async_copy(
            ref, lin_hbm.at[at, pl.ds(pl.multiple_of(side * 256, 256), 256)], sem
        )
        copy.start()
        return copy

    copies = [
        pltpu.make_async_copy(top_ref, win_hbm.at[pl.ds(0, WINDOW)], sems.at[5]),
        put(own_ref, half, pl.ds(0, f_ref.shape[1]), sems.at[4]),
    ]
    copies[0].start()
    for n, rows in enumerate(
        finish_half(1 - half, f_ref, e_ref, peer_ref, num_ref, den_ref, obuf, weights)
    ):
        copies.append(put(obuf.at[rows], 1 - half, rows, sems.at[n]))
    for copy in copies:
        copy.wait()


def call(kernel, out, *args, in_specs, after=(), flops=0, nbytes=0, vmem=8, **kw):
    given = len(args)

    def run(*refs):
        kernel(*refs[:given], *refs[given + len(after) :])

    return pl.pallas_call(
        run,
        out_shape=out,
        in_specs=list(in_specs) + [pl.BlockSpec(memory_space=pl.ANY)] * len(after),
        cost_estimate=pl.CostEstimate(flops=flops, bytes_accessed=nbytes, transcendentals=0),
        compiler_params=pltpu.CompilerParams(vmem_limit_bytes=vmem << 20),
        name=kernel.__name__,
        **kw,
    )(*args, *after)


def exchange(x, step):
    count = lax.axis_size("seq")
    return lax.ppermute(x, "seq", [(i, i ^ step) for i in range(count)])


def shape(*dims, dtype=BF):
    return jax.ShapeDtypeStruct(dims, dtype)


def body(q_lin, k_lin, v_lin, q_win, k_win, v_win):
    tok = q_lin.shape[0]
    count = lax.axis_size("seq")
    assert count & (count - 1) == 0 and count > 1
    me = lax.axis_index("seq")
    bits = [(me & (1 << n)) != 0 for n in range(count.bit_length() - 1)]
    bits, k_lin = lax.optimization_barrier((bits, k_lin))
    wide = WHEADS * WDIM
    hbm = pl.BlockSpec(memory_space=pltpu.HBM)

    state, key_edge, val_edge, q_lin, k_lin, v_lin, order = call(
        state_kernel,
        (
            shape(2, ROWS, 128),
            shape(WINDOW, wide),
            shape(WINDOW, wide),
            shape(*q_lin.shape),
            shape(*k_lin.shape),
            shape(*v_lin.shape),
            shape(128, (1 + PAIRS) * 256),
        ),
        *(pltpu.with_memory_space_constraint(x, pltpu.HBM) for x in (q_lin, k_lin, v_lin, k_win, v_win)),
        in_specs=[hbm] * 5,
        out_specs=(VMEM,) * 7,
        scratch_shapes=[pltpu.VMEM((2, tok, PAIRS * 128), BF), pltpu.SemaphoreType.DMA((5,))],
        flops=1 << 30,
        nbytes=2 << 20,
    )

    def ring(x, after):
        x, after = lax.optimization_barrier((x, after))
        return lax.ppermute(x, "seq", [(i, (i + 1) % count) for i in range(count)]), after

    peer = exchange(state, 1)
    token = shape(8, 128, dtype=F32)
    feats, first = call(
        query_kernel,
        (shape(2, tok, PAIRS * 128), token),
        q_lin,
        order,
        after=(state,),
        in_specs=[VMEM] * 2,
        out_specs=(VMEM, VMEM),
        flops=1 << 28,
        nbytes=2 << 20,
    )
    done = (first,)
    peer, done = lax.optimization_barrier((peer, done))
    both = state.astype(F32) + peer.astype(F32)
    carried = jnp.where(bits[0], both[1], both[0])
    before = jnp.zeros_like(carried)

    def local(after):
        num, den, done = call(
            local_kernel,
            (shape(2, tok, HEADS * VDIM // 2, dtype=F32),) * 2 + (token,),
            q_lin,
            k_lin,
            v_lin,
            after=after,
            in_specs=[VMEM] * 3,
            out_specs=(VMEM,) * 3,
            flops=1 << 31,
            nbytes=3 << 20,
        )
        return (num, den), (done,)

    def window(after):
        win, done = call(
            window_kernel,
            (shape(tok, wide), token),
            q_win,
            k_win,
            v_win,
            after=after,
            in_specs=[VMEM] * 3,
            out_specs=(VMEM, VMEM),
            flops=1 << 31,
            nbytes=8 << 20,
        )
        return win, (done,)

    def top(after, win):
        shares, win, done = call(
            top_kernel,
            (shape(WINDOW, wide), shape(tok, wide), token),
            q_win,
            k_win,
            v_win,
            key_edge,
            win,
            after=after,
            in_specs=[VMEM] * 5,
            out_specs=(VMEM, hbm, VMEM),
            scratch_shapes=[
                pltpu.VMEM((WINDOW, wide), BF),
                pltpu.SemaphoreType.DMA((2,)),
            ],
            flops=1 << 30,
            nbytes=2 << 20,
        )
        return shares, win, (done,)

    step, turn = 2, 0
    sums = win = shares = None
    while step < count:
        send = carried.astype(BF)
        if turn == 0:
            key_edge, send = ring(key_edge, send)
        elif turn == 1:
            val_edge, send = ring(val_edge, send)
        got = exchange(send, step + step // 2 if 2 * step == count else step)
        after = (send,) + done
        if turn == 0:
            sums, done = local(after)
        elif turn == 1:
            win, done = window(after)
        elif turn == 2:
            shares, win, done = top(after, win)
        if turn == 2:
            got, done, val_edge = lax.optimization_barrier((got, done, val_edge))
        elif turn < 2:
            got, done = lax.optimization_barrier((got, done))
        got = got.astype(F32)
        before = before + jnp.where(bits[turn + 1], got, 0.0)
        carried = carried + got
        step *= 2
        turn += 1
    assert turn >= 3
    own = before.astype(BF)
    other = exchange(own, 1)
    weights = pltpu.VMEM((PAIRS * 128, 256), BF)
    mine, top = call(
        own_kernel,
        (shape(tok, HEADS * VDIM // 2), shape(WINDOW, wide)),
        feats,
        own,
        peer,
        *sums,
        shares,
        v_win,
        val_edge,
        after=done,
        in_specs=[VMEM] * 8,
        out_specs=(VMEM, VMEM),
        scratch_shapes=[weights],
        flops=1 << 30,
        nbytes=3 << 20,
    )
    other, mine, top = lax.optimization_barrier((other, mine, top))
    return call(
        tail_kernel,
        (shape(tok, HEADS * VDIM), shape(tok, wide)),
        feats,
        other,
        peer,
        *sums,
        mine,
        top,
        win,
        in_specs=[VMEM] * 7 + [hbm],
        out_specs=(hbm, hbm),
        scratch_shapes=[
            weights,
            pltpu.VMEM((tok, HEADS * VDIM // 2), BF),
            pltpu.SemaphoreType.DMA((6,)),
        ],
        input_output_aliases={7: 1},
        flops=1 << 29,
        nbytes=2 << 20,
    )


def solution(mesh):
    spec = P(("groups", "seq"), None)
    return jax.shard_map(
        body, mesh=mesh, in_specs=(spec,) * 6, out_specs=(spec, spec), check_vma=False
    )
```
